128 devices in a mesh: ctx: 16 (over z, x), kvh: 8 (over y, core).
Axes of the slice: x: 4, y: 4, z: 4, core: 2. Of those that a mesh axis runs over, the one named last changes fastest.
Arguments:
- queries: bfloat16 [16384, 8192], P('ctx', 'kvh'), may hold values from -8 to 8
- keys: bfloat16 [16384, 1024], P(('ctx', 'kvh')), may hold values from -8 to 8
- values: bfloat16 [16384, 1024], P(('ctx', 'kvh')), may hold values from -6 to 6
- out_grad: bfloat16 [16384, 8192], P('ctx', 'kvh'), may hold values from -6 to 6
- random_blocks: int32 [128, 3], replicated, may hold values from 8 to 127, as said below
Outputs:
- attended: bfloat16 [16384, 8192], P('ctx', 'kvh')
- query_grad: bfloat16 [16384, 8192], P('ctx', 'kvh')
- key_grad: bfloat16 [16384, 1024], P(('ctx', 'kvh'))
- value_grad: bfloat16 [16384, 1024], P(('ctx', 'kvh'))
The draws below stay inside these ranges and needn't reach their ends.
Inputs may be any that keep to these rules, and one draw needn't show every extreme that they name: `random_blocks`: block b lies on ctx index b // 8. For each query block the 3 named blocks lie on 3 different ctx indices, none of them 0, the index holding the query block, or its two neighbours. Over the 8 rows of one ctx index, the named blocks (repeats counted) fall on 12 ctx indices as evenly as possible: none holds more than 2 of them and some holds exactly 2.
All inputs are finite; a program needn't handle non-finite values.
Results may differ from the reference program's by a relative error of at most 0.014.
Values may be sent and summed in bfloat16 or wider, within the bound.
A program may use at most 128 MiB of HBM per device.

```python
import math
import jax
import jax.numpy as jnp
from jax import lax

HD = 128
QPK = 8
KVH = 8
BLK = 128
GLOB = 2
RAND = 3
HEADS = 64
TOKENS = 16384
NKB = 128
QB_DEV = 8


def scale_rows(subkey, count_rows, count_cols):
    log_low = math.log(0.35)
    log_high = math.log(3.0)
    return jnp.exp(jax.random.uniform(subkey, (count_rows, count_cols, 1), jnp.float32, log_low, log_high))


def draw_queries(key, part):
    row_scales = scale_rows(jax.random.fold_in(key, 11), TOKENS, HEADS)
    entries = jax.random.normal(jax.random.fold_in(key, 13), (TOKENS, HEADS, HD), jnp.float32) * row_scales
    return jnp.clip(entries, -8.0, 8.0).reshape(TOKENS, HEADS * HD).astype(jnp.bfloat16)


def draw_keys(key, part):
    row_scales = scale_rows(jax.random.fold_in(key, 21), TOKENS, KVH)
    entries = jax.random.normal(jax.random.fold_in(key, 23), (TOKENS, KVH, HD), jnp.float32) * row_scales
    return jnp.clip(entries, -8.0, 8.0).reshape(TOKENS, KVH * HD).astype(jnp.bfloat16)


def shuffled(subkey, devices):
    return jax.random.permutation(subkey, devices)


def draw_random_blocks(key, part):
    devices = NKB // QB_DEV
    far_count = devices - 4
    slot_count = QB_DEV * RAND
    order_keys = jax.random.split(jax.random.fold_in(key, 31), devices)
    ranking = jax.vmap(lambda subkey: shuffled(subkey, devices))(order_keys)
    device_ids = jnp.arange(devices)
    nearby = (device_ids[None, :] == 0) | (jnp.abs(device_ids[None, :] - device_ids[:, None]) <= 1)
    scores = jnp.where(nearby, ranking + devices, ranking)
    ordering = jnp.argsort(scores, axis=1, stable=True)
    far_list = ordering[:, :far_count]
    slot_ids = jnp.arange(slot_count) % far_count
    owners = far_list[:, slot_ids]
    offsets = jax.random.randint(jax.random.fold_in(key, 32), (devices, slot_count), 0, QB_DEV)
    return (owners * QB_DEV + offsets).astype(jnp.int32).reshape(NKB, RAND)


def block_scale(stream_key, shape, cuts, low, top_value):
    def one(axis_at, shards_of):
        heights = jax.random.uniform(jax.random.fold_in(jax.random.fold_in(stream_key, 6), axis_at), (shards_of,), jnp.float32, low / len(cuts), top_value / len(cuts))
        return jnp.repeat(jnp.exp(heights), shape[axis_at] // shards_of).reshape((-1,) + (1,) * (len(shape) - axis_at - 1))

    gain = one(*cuts[0])
    for cut in cuts[1:]:
        gain = gain * one(*cut)
    return gain


def centred(rng, shape, deviation, reach, pieces=(), kind=jnp.bfloat16):
    factor_of = block_scale(rng, shape, pieces, -0.22, 0.18) if pieces else 1.0
    result = jax.random.normal(rng, shape, jnp.float32) * deviation * factor_of
    return jnp.minimum(jnp.maximum(result, -reach), reach).astype(kind)


def setup_inputs(seed: int = 0) -> dict:
    seeds = jax.random.split(jax.random.key(seed), 6)
    return {
        "queries": draw_queries(jax.random.fold_in(seeds[5], 71), 0),
        "keys": draw_keys(jax.random.fold_in(seeds[5], 71), 0),
        "values": centred(seeds[2], (TOKENS, KVH * HD), 1.0, 6.0, ((0, 128),)),
        "out_grad": centred(seeds[3], (TOKENS, HEADS * HD), 1.0, 6.0, ((0, 16), (1, 8))),
        "random_blocks": draw_random_blocks(jax.random.fold_in(seeds[5], 71), 0),
    }


def reference(queries, keys, values, out_grad, random_blocks):
    tokens = queries.shape[0]
    all_blocks = tokens // BLK
    score_scale = HD ** -0.5
    select_count = 3 + GLOB + RAND
    query_rows = queries.reshape(all_blocks, BLK, KVH, QPK, HD)
    grad_rows = out_grad.reshape(all_blocks, BLK, KVH, QPK, HD)
    key_blocks = keys.reshape(all_blocks, BLK, KVH, HD)
    value_blocks = values.reshape(all_blocks, BLK, KVH, HD)

    def visit_block(accums, step_items):
        key_acc, value_acc = accums
        block_index, query_here, grad_here, chosen = step_items
        window_ids = block_index - 1 + jnp.arange(3, dtype=jnp.int32)
        listed = jnp.concatenate([window_ids, jnp.arange(GLOB, dtype=jnp.int32), chosen.astype(jnp.int32)])
        usable = jnp.concatenate([(window_ids >= GLOB) & (window_ids < all_blocks), jnp.ones((GLOB + RAND,), jnp.bool_)])
        usable = jnp.repeat(usable, BLK)
        listed = jnp.clip(listed, 0, all_blocks - 1).astype(jnp.int32)
        key_rows = key_blocks[listed].reshape(select_count * BLK, KVH, HD).astype(jnp.float32)
        value_rows = value_blocks[listed].reshape(select_count * BLK, KVH, HD).astype(jnp.float32)
        query_f = query_here.astype(jnp.float32)
        grad_f = grad_here.astype(jnp.float32)
        scores = jnp.einsum("bgqd,kgd->gqbk", query_f, key_rows) * score_scale
        scores = jnp.where(usable, scores, -jnp.inf)
        largest = jnp.max(scores, axis=-1, keepdims=True)
        raised = jnp.exp(scores - largest)
        probs = raised / jnp.sum(raised, axis=-1, keepdims=True)
        weights = lax.optimization_barrier(probs.astype(jnp.bfloat16)).astype(jnp.float32)
        attended = jnp.einsum("gqbk,kgd->bgqd", weights, value_rows)
        prob_grad = jnp.einsum("bgqd,kgd->gqbk", grad_f, value_rows)
        centre = jnp.sum(probs * prob_grad, axis=-1, keepdims=True)
        score_grad = lax.optimization_barrier((probs * (prob_grad - centre) * score_scale).astype(jnp.bfloat16)).astype(jnp.float32)
        query_grad = jnp.einsum("gqbk,kgd->bgqd", score_grad, key_rows)
        key_grad = jnp.einsum("gqbk,bgqd->kgd", score_grad, query_f)
        value_grad = jnp.einsum("gqbk,bgqd->kgd", weights, grad_f)
        key_acc = key_acc.at[listed].add(key_grad.reshape(select_count, BLK, KVH, HD))
        value_acc = value_acc.at[listed].add(value_grad.reshape(select_count, BLK, KVH, HD))
        return (key_acc, value_acc), (attended.astype(jnp.bfloat16), query_grad.astype(jnp.bfloat16))

    zeros_acc = jnp.zeros((all_blocks, BLK, KVH, HD), jnp.float32)
    block_list = jnp.arange(all_blocks, dtype=jnp.int32)
    (key_acc, value_acc), (attended, query_grad) = lax.scan(visit_block, (zeros_acc, zeros_acc), (block_list, query_rows, grad_rows, random_blocks))
    return (attended.reshape(tokens, KVH * QPK * HD), query_grad.reshape(tokens, KVH * QPK * HD), key_acc.reshape(tokens, KVH * HD).astype(jnp.bfloat16), value_acc.reshape(tokens, KVH * HD).astype(jnp.bfloat16))
```

```python
import functools

import jax
import jax.numpy as jnp
from jax import lax
from jax.experimental import pallas as pl
from jax.experimental.pallas import tpu as pltpu
from jax.sharding import PartitionSpec as P

HD = 128
BLK = 128
GLOB = 2
RAND = 3
QB = 8
CTX = 16
KVH = 8
HEADS = 8
SLOTS = 2
NKB = QB * CTX
EXTRA = QB
RECV = QB + 1
POOL = RECV + CTX * SLOTS
ENTRIES = 3 + GLOB + RAND
CHUNK = 512
SCALE = HD**-0.5
LOG2E = 1.4426950408889634
MASKED = -1e30

NT = (((1,), (1,)), ((), ()))
TN = (((0,), (0,)), ((), ()))


def mm(a, b, dims=(((1,), (0,)), ((), ()))):
    return lax.dot_general(a, b, dims, preferred_element_type=jnp.float32)


def slot_blocks(rand, me, dest):
    first = jnp.int32(0)
    second = jnp.int32(0)
    count = jnp.int32(0)
    for e in range(QB * RAND):
        r = rand[dest * (QB * RAND) + e]
        hit = (r // QB) == me
        local = r % QB
        first = jnp.where(hit & (count == 0), local, first)
        second = jnp.where(hit & (count == 1), local, second)
        count = count + hit.astype(jnp.int32)
    first = jnp.where(dest == me + 1, QB - 1, first)
    first = jnp.where(me == 0, 0, first)
    second = jnp.where(me == 0, 1, second)
    return first, second


def pack_kernel(rand, kv_ref, out_ref):
    me = lax.axis_index("ctx")

    def body(dest, carry):
        for k, local in enumerate(slot_blocks(rand, me, dest)):
            for t in range(2):
                out_ref[dest, k, t] = kv_ref[t, local]
        return carry

    lax.fori_loop(0, CTX, body, 0)


def attend_kernel(
    rand, q_ref, g_ref, kv_ref, recv_ref, extra_ref,
    o_ref, dq_ref, local_ref, back_ref, back_extra_ref,
    pool, grads, kall, vall, dk, dv, table, fill,
):
    me = lax.axis_index("ctx")
    i = pl.program_id(0)

    @pl.when(i == 0)
    def _():
        for t in range(2):
            for b in range(QB):
                pool[b, t] = kv_ref[t, b]
            pool[EXTRA, t] = extra_ref[t]
        for s in range(CTX):
            for k in range(SLOTS):
                for t in range(2):
                    pool[RECV + s * SLOTS + k, t] = recv_ref[s, k, t]
        grads[...] = jnp.zeros_like(grads)
        for s in range(CTX):
            fill[s] = 0

    for e in range(3):
        gid = me * QB + i - 1 + e
        near = i - 1 + e
        before = jnp.where(me == 1, EXTRA, RECV + (me - 1) * SLOTS)
        after = RECV + (me + 1) * SLOTS
        place = jnp.where(near < 0, before, jnp.where(near >= QB, after, near))
        ok = (gid >= GLOB) & (gid < NKB)
        table[e] = jnp.where(ok, place, 0)
    for e in range(GLOB):
        table[3 + e] = jnp.where(me == 0, e, RECV + e)
    for e in range(RAND):
        r = rand[(me * QB + i) * RAND + e]
        owner = r // QB
        rank = fill[owner]
        fill[owner] = rank + 1
        table[3 + GLOB + e] = RECV + owner * SLOTS + rank

    for e in range(ENTRIES):
        kall[e * BLK : (e + 1) * BLK, :] = pool[table[e], 0]
        vall[e * BLK : (e + 1) * BLK, :] = pool[table[e], 1]
    dk[...] = jnp.zeros_like(dk)
    dv[...] = jnp.zeros_like(dv)
    per = CHUNK // BLK

    def chunk(j, carry):
        cols = [pl.ds(pl.multiple_of((j * per + t) * HD, HD), HD) for t in range(per)]
        q = jnp.concatenate([q_ref[:, c] for c in cols], 0)
        g = jnp.concatenate([g_ref[:, c] for c in cols], 0)
        s = mm(q, kall[...], NT)
        parts = []
        for e in range(ENTRIES):
            part = s[:, e * BLK : (e + 1) * BLK]
            if e < 3:
                gid = me * QB + i - 1 + e
                ok = (gid >= GLOB) & (gid < NKB)
                part = part + jnp.where(ok, 0.0, MASKED).astype(jnp.float32)
            parts.append(part)
        s = jnp.concatenate(parts, 1)
        top = jnp.max(s, 1, keepdims=True)
        p = jnp.exp2(s * (SCALE * LOG2E) - top * (SCALE * LOG2E))
        inv = 1.0 / jnp.sum(p, 1, keepdims=True)
        pb = p.astype(jnp.bfloat16)
        o = mm(pb, vall[...]) * inv
        gb = (g.astype(jnp.float32) * inv).astype(jnp.bfloat16)
        centre = jnp.sum(gb.astype(jnp.float32) * o, 1, keepdims=True)
        dp = mm(gb, vall[...], NT)
        ds = (p * (dp - centre)).astype(jnp.bfloat16)
        dq = mm(ds, kall[...]) * SCALE
        for t in range(per):
            rows = slice(t * BLK, (t + 1) * BLK)
            o_ref[:, cols[t]] = o[rows].astype(jnp.bfloat16)
            dq_ref[:, cols[t]] = dq[rows].astype(jnp.bfloat16)
        dv[...] += mm(gb, pb, TN)
        dk[...] += mm(q, ds, TN)
        return carry

    lax.fori_loop(0, HEADS * BLK // CHUNK, chunk, 0)
    for e in range(ENTRIES):
        cols = slice(e * BLK, (e + 1) * BLK)
        grads[table[e], 0] = grads[table[e], 0] + dk[:, cols] * SCALE
        grads[table[e], 1] = grads[table[e], 1] + dv[:, cols]

    @pl.when(i == QB - 1)
    def _():
        for t in range(2):
            for b in range(QB):
                local_ref[b, t] = grads[b, t]
            back_extra_ref[t] = grads[EXTRA, t].astype(jnp.bfloat16)
        for s in range(CTX):
            for k in range(SLOTS):
                for t in range(2):
                    back_ref[s, k, t] = grads[RECV + s * SLOTS + k, t].astype(jnp.bfloat16)


def total_kernel(rand, local_ref, back_ref, extra_ref, out_ref, acc):
    me = lax.axis_index("ctx")
    acc[...] = local_ref[...]

    def body(src, carry):
        for k, local in enumerate(slot_blocks(rand, me, src)):
            for t in range(2):
                acc[local, t] = acc[local, t] + back_ref[src, k, t].astype(jnp.float32)
        return carry

    lax.fori_loop(0, CTX, body, 0)
    for t in range(2):
        acc[QB - 1, t] = acc[QB - 1, t] + extra_ref[t].astype(jnp.float32)
    for t in range(2):
        for b in range(QB):
            out_ref[t, b] = acc[b, t].T.astype(jnp.bfloat16)


VM = pl.BlockSpec(memory_space=pltpu.VMEM)
SM = pl.BlockSpec(memory_space=pltpu.SMEM)
BIG = pltpu.CompilerParams(vmem_limit_bytes=56 * 2**20)


def per_device(queries, keys, values, out_grad, random_blocks):
    rand = random_blocks.reshape(-1)
    bf = jnp.bfloat16
    stacked = jnp.stack([keys, values])
    kv = lax.all_to_all(stacked, "kvh", split_axis=2, concat_axis=1, tiled=True)
    kv = kv.reshape(2, QB, BLK, HD)
    extra = lax.ppermute(kv[:, QB - 1], "ctx", [(0, 1)])
    send = pl.pallas_call(
        pack_kernel,
        out_shape=jax.ShapeDtypeStruct((CTX, SLOTS, 2, BLK, HD), bf),
        in_specs=[SM, VM],
        out_specs=VM,
        compiler_params=BIG,
    )(rand, kv)
    recv = lax.all_to_all(send, "ctx", split_axis=0, concat_axis=0, tiled=True)
    whole = lambda shape: pl.BlockSpec(shape, lambda i, *_: (0,) * len(shape))
    rows = pl.BlockSpec((BLK, HEADS * HD), lambda i, *_: (i, 0))
    tok = QB * BLK
    attended, query_grad, local, back, back_extra = pl.pallas_call(
        attend_kernel,
        grid_spec=pltpu.PrefetchScalarGridSpec(
            num_scalar_prefetch=1,
            grid=(QB,),
            in_specs=[
                rows,
                rows,
                whole((2, QB, BLK, HD)),
                whole((CTX, SLOTS, 2, BLK, HD)),
                whole((2, BLK, HD)),
            ],
            out_specs=[
                rows,
                rows,
                whole((QB, 2, HD, BLK)),
                whole((CTX, SLOTS, 2, HD, BLK)),
                whole((2, HD, BLK)),
            ],
            scratch_shapes=[
                pltpu.VMEM((POOL, 2, BLK, HD), bf),
                pltpu.VMEM((POOL, 2, HD, BLK), jnp.float32),
                pltpu.VMEM((ENTRIES * BLK, HD), bf),
                pltpu.VMEM((ENTRIES * BLK, HD), bf),
                pltpu.VMEM((HD, ENTRIES * BLK), jnp.float32),
                pltpu.VMEM((HD, ENTRIES * BLK), jnp.float32),
                pltpu.SMEM((ENTRIES,), jnp.int32),
                pltpu.SMEM((CTX,), jnp.int32),
            ],
        ),
        out_shape=[
            jax.ShapeDtypeStruct((tok, HEADS * HD), bf),
            jax.ShapeDtypeStruct((tok, HEADS * HD), bf),
            jax.ShapeDtypeStruct((QB, 2, HD, BLK), jnp.float32),
            jax.ShapeDtypeStruct((CTX, SLOTS, 2, HD, BLK), bf),
            jax.ShapeDtypeStruct((2, HD, BLK), bf),
        ],
        compiler_params=BIG,
    )(rand, queries, out_grad, kv, recv, extra)
    back = lax.all_to_all(back, "ctx", split_axis=0, concat_axis=0, tiled=True)
    back_extra = lax.ppermute(back_extra, "ctx", [(1, 0)])
    total = pl.pallas_call(
        total_kernel,
        out_shape=jax.ShapeDtypeStruct((2, QB, BLK, HD), bf),
        in_specs=[SM, VM, VM, VM],
        out_specs=VM,
        scratch_shapes=[pltpu.VMEM((QB, 2, HD, BLK), jnp.float32)],
        compiler_params=BIG,
    )(rand, local, back, back_extra)
    home = lax.all_to_all(
        total.reshape(2, tok, HD), "kvh", split_axis=1, concat_axis=2, tiled=True
    )
    return attended, query_grad, home[0], home[1]


def solution(mesh):
    in_specs = (
        P("ctx", "kvh"),
        P(("ctx", "kvh"), None),
        P(("ctx", "kvh"), None),
        P("ctx", "kvh"),
        P(),
    )
    out_specs = (P("ctx", "kvh"), P("ctx", "kvh"), P(("ctx", "kvh"), None), P(("ctx", "kvh"), None))
    return jax.shard_map(
        per_device, mesh=mesh, in_specs=in_specs, out_specs=out_specs, check_vma=False
    )
```

```python
import functools

import jax
import jax.numpy as jnp
from jax import lax
from jax.experimental import pallas as pl
from jax.experimental.pallas import tpu as pltpu
from jax.sharding import PartitionSpec as P

HD = 128
BLK = 128
GLOB = 2
RAND = 3
QB = 8
CTX = 16
KVH = 8
HEADS = 8
SLOTS = 2
NKB = QB * CTX
SIDE = 4
EXTRA = QB
RECV = QB + 1
POOL = RECV + CTX * SLOTS
ENTRIES = 3 + GLOB + RAND
CHUNK = 512
SCALE = HD**-0.5
LOG2E = 1.4426950408889634
MASKED = -1e30
MESH = pl.DeviceIdType.MESH
ORDER = (
    (0, 1), (1, 0), (0, 3), (3, 0), (1, 1), (2, 0), (3, 3), (0, 2),
    (1, 3), (2, 1), (3, 1), (1, 2), (2, 3), (3, 2), (2, 2),
)

NT = (((1,), (1,)), ((), ()))
TN = (((0,), (0,)), ((), ()))


def mm(a, b, dims=(((1,), (0,)), ((), ()))):
    return lax.dot_general(a, b, dims, preferred_element_type=jnp.float32)


def ctx_at(me, dz, dx):
    return lax.rem(me // SIDE + dz, SIDE) * SIDE + lax.rem(me % SIDE + dx, SIDE)


def slot_table(rand, me, table):
    def body(dest, carry):
        first = second = count = jnp.int32(0)
        for e in range(QB * RAND):
            r = rand[dest * (QB * RAND) + e]
            hit = (r >> 3) == me
            first = jnp.where(hit & (count == 0), r & 7, first)
            second = jnp.where(hit & (count == 1), r & 7, second)
            count = count + hit.astype(jnp.int32)
        first = jnp.where(dest == me + 1, QB - 1, first)
        table[dest * 2] = jnp.where(me == 0, 0, first)
        table[dest * 2 + 1] = jnp.where(me == 0, 1, second)
        return carry

    lax.fori_loop(0, CTX, body, 0)


def greet(me, h):
    barrier = pltpu.get_barrier_semaphore()
    for dz, dx in ORDER:
        peer = (ctx_at(me, dz, dx), h)
        pl.semaphore_signal(barrier, inc=1, device_id=peer, device_id_type=MESH)
    for dh in range(1, KVH):
        peer = (me, lax.rem(h + dh, KVH))
        pl.semaphore_signal(barrier, inc=1, device_id=peer, device_id_type=MESH)
    pl.semaphore_wait(barrier, CTX + KVH - 2)


def remote(src, dst, send, recv, peer):
    return pltpu.make_async_remote_copy(
        src_ref=src, dst_ref=dst, send_sem=send, recv_sem=recv, device_id=peer, device_id_type=MESH
    )


def gather_kernel(
    rand, key_ref, value_ref, pool_ref, table_ref,
    local_k, local_v, packed, head_send, head_recv, ctx_send, ctx_recv, extra_sem, own_sem, keep_sem,
):
    me = lax.axis_index("ctx")
    h = lax.axis_index("kvh")
    greet(me, h)
    local = (local_k, local_v)
    cols = lambda head: pl.ds(pl.multiple_of(head * HD, HD), HD)
    head_copies = []
    own_copies = []
    for t, ref in enumerate((key_ref, value_ref)):
        for dh in range(1, KVH):
            peer = lax.rem(h + dh, KVH)
            head_copies.append(
                remote(
                    ref.at[:, cols(peer)], local[t].at[h],
                    head_send.at[t, peer], head_recv.at[t, h], (me, peer),
                )
            )
            head_copies[-1].start()
        own_copies.append(
            pltpu.make_async_copy(ref.at[:, cols(h)], local[t].at[h], own_sem.at[t])
        )
        own_copies[-1].start()
    slot_table(rand, me, table_ref)
    keep_copies = []
    ctx_copies = []
    for t in range(2):
        own_copies[t].wait()
        for dh in range(1, KVH):
            peer = lax.rem(h + dh, KVH)
            remote(
                local[t].at[peer], local[t].at[peer],
                head_send.at[t, peer], head_recv.at[t, peer], (me, peer),
            ).wait_recv()
        keep_copies.append(
            pltpu.make_async_copy(local[t], pool_ref.at[t, pl.ds(0, QB)], keep_sem.at[t])
        )
        keep_copies[-1].start()
        for dz, dx in ORDER:
            peer = ctx_at(me, dz, dx)
            for k in range(SLOTS):
                packed[t, peer, k] = local[t][table_ref[peer * 2 + k]]
        for dz, dx in ORDER:
            peer = ctx_at(me, dz, dx)
            ctx_copies.append(
                remote(
                    packed.at[t, peer], pool_ref.at[t, pl.ds(RECV + me * SLOTS, SLOTS)],
                    ctx_send.at[t, peer], ctx_recv.at[t, me], (peer, h),
                )
            )
            ctx_copies[-1].start()

    def extra(t):
        return remote(
            local[t].at[QB - 1], pool_ref.at[t, EXTRA], extra_sem.at[0, t], extra_sem.at[1, t], (1, h)
        )

    @pl.when(me == 0)
    def _():
        for t in range(2):
            extra(t).start()
        for t in range(2):
            extra(t).wait_send()

    @pl.when(me == 1)
    def _():
        for t in range(2):
            remote(
                local[t].at[QB - 1], pool_ref.at[t, EXTRA],
                extra_sem.at[0, t], extra_sem.at[1, t], (0, h),
            ).wait_recv()

    for copy in head_copies:
        copy.wait_send()
    for copy in keep_copies:
        copy.wait()
    for copy in ctx_copies:
        copy.wait_send()
    for t in range(2):
        for dz, dx in ORDER:
            peer = ctx_at(me, dz, dx)
            remote(
                packed.at[t, peer], pool_ref.at[t, pl.ds(RECV + peer * SLOTS, SLOTS)],
                ctx_send.at[t, peer], ctx_recv.at[t, peer], (peer, h),
            ).wait_recv()


def attend_kernel(
    rand, q_ref, g_ref, pool,
    o_ref, dq_ref, local_ref, back_ref, back_extra_ref,
    grads, kall, vall, dk, dv, table, fill,
):
    me = lax.axis_index("ctx")
    i = pl.program_id(0)

    @pl.when(i == 0)
    def _():
        grads[...] = jnp.zeros_like(grads)
        back_ref[...] = jnp.zeros_like(back_ref)
        for s in range(CTX):
            fill[s] = 0

    for e in range(3):
        gid = me * QB + i - 1 + e
        near = i - 1 + e
        before = jnp.where(me == 1, EXTRA, RECV + (me - 1) * SLOTS)
        after = RECV + (me + 1) * SLOTS
        place = jnp.where(near < 0, before, jnp.where(near >= QB, after, near))
        ok = (gid >= GLOB) & (gid < NKB)
        table[e] = jnp.where(ok, place, 0)
    for e in range(GLOB):
        table[3 + e] = jnp.where(me == 0, e, RECV + e)
    for e in range(RAND):
        r = rand[(me * QB + i) * RAND + e]
        owner = r >> 3
        rank = fill[owner]
        fill[owner] = rank + 1
        table[3 + GLOB + e] = RECV + owner * SLOTS + rank

    for e in range(ENTRIES):
        kall[e * BLK : (e + 1) * BLK, :] = pool[0, table[e]]
        vall[e * BLK : (e + 1) * BLK, :] = pool[1, table[e]]
    dk[...] = jnp.zeros_like(dk)
    dv[...] = jnp.zeros_like(dv)
    per = CHUNK // BLK

    def chunk(j, carry):
        cols = [pl.ds(pl.multiple_of((j * per + t) * HD, HD), HD) for t in range(per)]
        q = jnp.concatenate([q_ref[:, c] for c in cols], 0)
        g = jnp.concatenate([g_ref[:, c] for c in cols], 0)
        s = mm(q, kall[...], NT)
        parts = []
        for e in range(ENTRIES):
            part = s[:, e * BLK : (e + 1) * BLK]
            if e < 3:
                gid = me * QB + i - 1 + e
                ok = (gid >= GLOB) & (gid < NKB)
                part = part + jnp.where(ok, 0.0, MASKED).astype(jnp.float32)
            parts.append(part)
        s = jnp.concatenate(parts, 1)
        top = jnp.max(s, 1, keepdims=True)
        p = jnp.exp2(s * (SCALE * LOG2E) - top * (SCALE * LOG2E))
        inv = 1.0 / jnp.sum(p, 1, keepdims=True)
        pb = p.astype(jnp.bfloat16)
        o = mm(pb, vall[...]) * inv
        gb = (g.astype(jnp.float32) * inv).astype(jnp.bfloat16)
        centre = jnp.sum(gb.astype(jnp.float32) * o, 1, keepdims=True)
        dp = mm(gb, vall[...], NT)
        ds = (p * (dp - centre)).astype(jnp.bfloat16)
        dq = mm(ds, kall[...]) * SCALE
        for t in range(per):
            rows = slice(t * BLK, (t + 1) * BLK)
            o_ref[:, cols[t]] = o[rows].astype(jnp.bfloat16)
            dq_ref[:, cols[t]] = dq[rows].astype(jnp.bfloat16)
        dv[...] += mm(gb, pb, TN)
        dk[...] += mm(q, ds, TN)
        return carry

    lax.fori_loop(0, HEADS * BLK // CHUNK, chunk, 0)
    for e in range(ENTRIES):
        cols = slice(e * BLK, (e + 1) * BLK)
        key_part = dk[:, cols] * SCALE
        value_part = dv[:, cols]
        if e < 3 + GLOB:
            grads[0, table[e]] += key_part
            grads[1, table[e]] += value_part
        else:
            slot = table[e] - RECV
            back_ref[0, slot] = key_part.astype(jnp.bfloat16)
            back_ref[1, slot] = value_part.astype(jnp.bfloat16)

    @pl.when(i == QB - 1)
    def _():
        for t in range(2):
            for b in range(QB):
                local_ref[t, b] = grads[t, b]
            back_extra_ref[t] = grads[t, EXTRA].astype(jnp.bfloat16)

        def shared(src):
            for t in range(2):
                for k in range(SLOTS):
                    slot = src * SLOTS + k
                    back_ref[t, slot] = grads[t, RECV + slot].astype(jnp.bfloat16)

        pl.when(me != 0)(lambda: shared(0))
        pl.when(me > 1)(lambda: shared(me - 1))
        pl.when(me < CTX - 1)(lambda: shared(me + 1))


def scatter_kernel(
    table, local_ref, back_ref, extra_ref, dk_ref, dv_ref,
    acc, arrived, extra_in, stage, ctx_send, ctx_recv, head_send, head_recv, extra_sem, own_sem,
):
    me = lax.axis_index("ctx")
    h = lax.axis_index("kvh")
    greet(me, h)
    ctx_copies = []
    for t in (1, 0):
        for dz, dx in ORDER:
            peer = ctx_at(me, dz, dx)
            ctx_copies.append(
                remote(
                    back_ref.at[t, pl.ds(peer * SLOTS, SLOTS)], arrived.at[t, me],
                    ctx_send.at[t, peer], ctx_recv.at[t, me], (peer, h),
                )
            )
            ctx_copies[-1].start()

    def extra(t, peer):
        return remote(extra_ref.at[t], extra_in.at[t], extra_sem.at[0, t], extra_sem.at[1, t], (peer, h))

    @pl.when(me == 1)
    def _():
        for t in range(2):
            extra(t, 0).start()

    acc[...] = local_ref[...]
    cols = lambda head: pl.ds(pl.multiple_of(head * HD, HD), HD)
    head_copies = []
    own_copies = []
    for t, ref in ((1, dv_ref), (0, dk_ref)):

        def body(n, carry):
            peer = lax.rem(me + n, CTX)
            remote(
                back_ref.at[t, pl.ds(peer * SLOTS, SLOTS)], arrived.at[t, peer],
                ctx_send.at[t, peer], ctx_recv.at[t, peer], (peer, h),
            ).wait_recv()
            for k in range(SLOTS):
                place = table[peer * 2 + k]
                term = arrived[t, peer, k].astype(jnp.float32)
                for b in range(QB):
                    acc[t, b] += term * (place == b).astype(jnp.float32)
            return carry

        lax.fori_loop(1, CTX, body, 0)

        @pl.when(me == 0)
        def _():
            extra(t, 1).wait_recv()
            acc[t, QB - 1] += extra_in[t].astype(jnp.float32)

        for b in range(QB):
            stage[t, b] = acc[t, b].T.astype(jnp.bfloat16)
        for dh in range(1, KVH):
            peer = lax.rem(h + dh, KVH)
            head_copies.append(
                remote(
                    stage.at[t, peer], ref.at[:, cols(h)],
                    head_send.at[t, peer], head_recv.at[t, h], (me, peer),
                )
            )
            head_copies[-1].start()
        own_copies.append(pltpu.make_async_copy(stage.at[t, h], ref.at[:, cols(h)], own_sem.at[t]))
        own_copies[-1].start()

    @pl.when(me == 1)
    def _():
        for t in range(2):
            extra(t, 0).wait_send()

    for copy in ctx_copies:
        copy.wait_send()
    for copy in own_copies:
        copy.wait()
    for copy in head_copies:
        copy.wait_send()
    for t, ref in ((1, dv_ref), (0, dk_ref)):
        for dh in range(1, KVH):
            peer = lax.rem(h + dh, KVH)
            remote(
                stage.at[t, peer], ref.at[:, cols(peer)],
                head_send.at[t, peer], head_recv.at[t, peer], (me, peer),
            ).wait_recv()


VM = pl.BlockSpec(memory_space=pltpu.VMEM)
SM = pl.BlockSpec(memory_space=pltpu.SMEM)
ANY = pl.BlockSpec(memory_space=pl.ANY)
DMA = pltpu.SemaphoreType.DMA
VMEM_BYTES = 56 * 2**20


def per_device(queries, keys, values, out_grad, random_blocks):
    rand = random_blocks.reshape(-1)
    bf = jnp.bfloat16
    pool, table = pl.pallas_call(
        gather_kernel,
        out_shape=[
            jax.ShapeDtypeStruct((2, POOL, BLK, HD), bf),
            jax.ShapeDtypeStruct((CTX * SLOTS,), jnp.int32),
        ],
        in_specs=[SM, ANY, ANY],
        out_specs=[ANY, SM],
        scratch_shapes=[
            pltpu.VMEM((QB, BLK, HD), bf),
            pltpu.VMEM((QB, BLK, HD), bf),
            pltpu.VMEM((2, CTX, SLOTS, BLK, HD), bf),
            DMA((2, KVH)), DMA((2, KVH)), DMA((2, CTX)), DMA((2, CTX)), DMA((2, 2)), DMA((2,)), DMA((2,)),
        ],
        compiler_params=pltpu.CompilerParams(
            collective_id=0, has_side_effects=True, vmem_limit_bytes=VMEM_BYTES
        ),
    )(rand, keys, values)
    whole = lambda shape: pl.BlockSpec(shape, lambda i, *_: (0,) * len(shape))
    rows = pl.BlockSpec((BLK, HEADS * HD), lambda i, *_: (i, 0))
    tok = QB * BLK
    attended, query_grad, local, back, back_extra = pl.pallas_call(
        attend_kernel,
        grid_spec=pltpu.PrefetchScalarGridSpec(
            num_scalar_prefetch=1,
            grid=(QB,),
            in_specs=[rows, rows, whole((2, POOL, BLK, HD))],
            out_specs=[
                rows,
                rows,
                whole((2, QB, HD, BLK)),
                whole((2, CTX * SLOTS, HD, BLK)),
                whole((2, HD, BLK)),
            ],
            scratch_shapes=[
                pltpu.VMEM((2, POOL, HD, BLK), jnp.float32),
                pltpu.VMEM((ENTRIES * BLK, HD), bf),
                pltpu.VMEM((ENTRIES * BLK, HD), bf),
                pltpu.VMEM((HD, ENTRIES * BLK), jnp.float32),
                pltpu.VMEM((HD, ENTRIES * BLK), jnp.float32),
                pltpu.SMEM((ENTRIES,), jnp.int32),
                pltpu.SMEM((CTX,), jnp.int32),
            ],
        ),
        out_shape=[
            jax.ShapeDtypeStruct((tok, HEADS * HD), bf),
            jax.ShapeDtypeStruct((tok, HEADS * HD), bf),
            jax.ShapeDtypeStruct((2, QB, HD, BLK), jnp.float32),
            jax.ShapeDtypeStruct((2, CTX * SLOTS, HD, BLK), bf),
            jax.ShapeDtypeStruct((2, HD, BLK), bf),
        ],
        compiler_params=pltpu.CompilerParams(vmem_limit_bytes=VMEM_BYTES),
    )(rand, queries, out_grad, pool)
    key_grad, value_grad = pl.pallas_call(
        scatter_kernel,
        out_shape=[jax.ShapeDtypeStruct((BLK, KVH * HD), bf)] * 2,
        in_specs=[SM, VM, ANY, ANY],
        out_specs=[ANY, ANY],
        scratch_shapes=[
            pltpu.VMEM((2, QB, HD, BLK), jnp.float32),
            pltpu.VMEM((2, CTX, SLOTS, HD, BLK), bf),
            pltpu.VMEM((2, HD, BLK), bf),
            pltpu.VMEM((2, QB, BLK, HD), bf),
            DMA((2, CTX)), DMA((2, CTX)), DMA((2, KVH)), DMA((2, KVH)), DMA((2, 2)), DMA((2,)),
        ],
        compiler_params=pltpu.CompilerParams(
            collective_id=1, has_side_effects=True, vmem_limit_bytes=VMEM_BYTES
        ),
    )(table, local, back, back_extra)
    return attended, query_grad, key_grad, value_grad


def solution(mesh):
    in_specs = (
        P("ctx", "kvh"),
        P(("ctx", "kvh"), None),
        P(("ctx", "kvh"), None),
        P("ctx", "kvh"),
        P(),
    )
    out_specs = (P("ctx", "kvh"), P("ctx", "kvh"), P(("ctx", "kvh"), None), P(("ctx", "kvh"), None))
    return jax.shard_map(
        per_device, mesh=mesh, in_specs=in_specs, out_specs=out_specs, check_vma=False
    )
```

```python
import functools

import jax
import jax.numpy as jnp
from jax import lax
from jax.experimental import pallas as pl
from jax.experimental.pallas import tpu as pltpu
from jax.sharding import PartitionSpec as P

HD = 128
BLK = 128
GLOB = 2
RAND = 3
QB = 8
CTX = 16
KVH = 8
HEADS = 8
SLOTS = 2
NKB = QB * CTX
SIDE = 4
EXTRA = QB
RECV = QB + 1
POOL = RECV + CTX * SLOTS
ENTRIES = 3 + GLOB + RAND
CHUNK = 512
PER = CHUNK // BLK
HALVES = HEADS // PER
NAMED = QB * RAND
EDGE = NAMED + GLOB
NONE = EDGE + 2
SUMS = QB + 2 + GLOB
SCALE = HD**-0.5
LOG2E = 1.4426950408889634
MASKED = -1e30
MESH = pl.DeviceIdType.MESH
ORDER = (
    (0, 1), (1, 0), (0, 3), (3, 0), (1, 1), (2, 0), (3, 3), (0, 2),
    (1, 3), (2, 1), (3, 1), (1, 2), (2, 3), (3, 2), (2, 2),
)

NT = (((1,), (1,)), ((), ()))
TN = (((0,), (0,)), ((), ()))


def mm(a, b, dims=(((1,), (0,)), ((), ()))):
    return lax.dot_general(a, b, dims, preferred_element_type=jnp.float32)


def ctx_at(me, dz, dx):
    return lax.rem(me // SIDE + dz, SIDE) * SIDE + lax.rem(me % SIDE + dx, SIDE)


def pick(rand, row, owner, name):
    first = second = jnp.int32(name(None, None))
    count = jnp.int32(0)
    for n in range(NAMED):
        r = rand[row * NAMED + n]
        hit = (r >> 3) == owner
        first = jnp.where(hit & (count == 0), name(r, n), first)
        second = jnp.where(hit & (count == 1), name(r, n), second)
        count = count + hit.astype(jnp.int32)
    return first, second


def send_table(rand, me, table):
    def body(dest, carry):
        first, second = pick(rand, dest, me, lambda r, n: 0 if r is None else r & 7)
        first = jnp.where(dest == me + 1, QB - 1, first)
        table[dest * 2] = jnp.where(me == 0, 0, first)
        table[dest * 2 + 1] = jnp.where(me == 0, 1, second)
        return carry

    lax.fori_loop(0, CTX, body, 0)


def back_table(rand, me, table):
    def body(src, carry):
        first, second = pick(rand, me, src, lambda r, n: NONE if r is None else n)
        first = jnp.where(src == me - 1, EDGE, first)
        first = jnp.where(src == me + 1, EDGE + 1, first)
        table[src * 2] = jnp.where(src == 0, NAMED, first)
        table[src * 2 + 1] = jnp.where(src == 0, NAMED + 1, second)
        return carry

    lax.fori_loop(0, CTX, body, 0)


def place_table(rand, me, table):
    def body(i, carry):
        for e in range(3):
            gid = me * QB + i - 1 + e
            near = i - 1 + e
            before = jnp.where(me == 1, EXTRA, RECV + (me - 1) * SLOTS)
            after = RECV + (me + 1) * SLOTS
            place = jnp.where(near < 0, before, jnp.where(near >= QB, after, near))
            ok = (gid >= GLOB) & (gid < NKB)
            table[i * ENTRIES + e] = jnp.where(ok, place, 0)
        for e in range(GLOB):
            table[i * ENTRIES + 3 + e] = jnp.where(me == 0, e, RECV + e)
        for e in range(RAND):
            owner = rand[me * NAMED + i * RAND + e] >> 3
            rank = jnp.int32(0)
            for n in range(NAMED):
                same = ((rand[me * NAMED + n] >> 3) == owner) & (n < i * RAND + e)
                rank = rank + same.astype(jnp.int32)
            table[i * ENTRIES + 3 + GLOB + e] = RECV + owner * SLOTS + rank
        return carry

    lax.fori_loop(0, QB, body, 0)


def greet(me, h):
    barrier = pltpu.get_barrier_semaphore()
    for dz, dx in ORDER:
        peer = (ctx_at(me, dz, dx), h)
        pl.semaphore_signal(barrier, inc=1, device_id=peer, device_id_type=MESH)
    for dh in range(1, KVH):
        peer = (me, lax.rem(h + dh, KVH))
        pl.semaphore_signal(barrier, inc=1, device_id=peer, device_id_type=MESH)
    pl.semaphore_wait(barrier, CTX + KVH - 2)


def remote(src, dst, send, recv, peer):
    return pltpu.make_async_remote_copy(
        src_ref=src, dst_ref=dst, send_sem=send, recv_sem=recv, device_id=peer, device_id_type=MESH
    )


def step_kernel(
    rand, q_hbm, g_hbm, key_ref, value_ref,
    o_hbm, dq_hbm, dk_ref, dv_ref,
    q, g, o, dq, probs, inverse, local_k, local_v, pool_k, pool_v, packed_k, packed_v, back_k, back_v,
    arrived_k, arrived_v, terms_k, terms_v, sums_k, sums_v, stage_k, stage_v, extra_k, extra_v,
    listed, part, outgoing, returning, places,
    head_send, head_recv, ctx_send, ctx_recv, home_send, home_recv, ret_send, ret_recv,
    extra_send, extra_recv, own_sem, home_own, in_sem, out_sem,
):
    me = lax.axis_index("ctx")
    h = lax.axis_index("kvh")
    bf = jnp.bfloat16
    pools, packs, backs = (pool_k, pool_v), (packed_k, packed_v), (back_k, back_v)
    local = (local_k, local_v)
    arrived, terms, sums = (arrived_k, arrived_v), (terms_k, terms_v), (sums_k, sums_v)
    stages, extras = (stage_k, stage_v), (extra_k, extra_v)
    loads = [
        pltpu.make_async_copy(q_hbm, q, in_sem.at[0]),
        pltpu.make_async_copy(g_hbm, g, in_sem.at[1]),
    ]
    for copy in loads:
        copy.start()
    greet(me, h)
    cols = lambda head: pl.ds(pl.multiple_of(head * HD, HD), HD)
    heads = lambda: [(dh, lax.rem(h + dh, KVH)) for dh in range(1, KVH)]
    peers = lambda: [ctx_at(me, dz, dx) for dz, dx in ORDER]
    sent = []
    own = []
    for t, ref in enumerate((key_ref, value_ref)):
        for _, peer in heads():
            sent.append(
                remote(
                    ref.at[:, cols(peer)], local[t].at[h],
                    head_send.at[t, peer], head_recv.at[t, h], (me, peer),
                )
            )
            sent[-1].start()
        own.append(pltpu.make_async_copy(ref.at[:, cols(h)], local[t].at[h], own_sem.at[t]))
        own[-1].start()
    send_table(rand, me, outgoing)
    for t in range(2):
        own[t].wait()
        for _, peer in heads():
            remote(
                local[t].at[peer], local[t].at[peer],
                head_send.at[t, peer], head_recv.at[t, peer], (me, peer),
            ).wait_recv()
        for peer in peers():
            for k in range(SLOTS):
                packs[t][peer, k] = local[t][outgoing[peer * 2 + k]]
        for peer in peers():
            sent.append(
                remote(
                    packs[t].at[peer], pools[t].at[pl.ds(RECV + me * SLOTS, SLOTS)],
                    ctx_send.at[t, peer], ctx_recv.at[t, me], (peer, h),
                )
            )
            sent[-1].start()

        @pl.when(me == 0)
        def _():
            remote(
                local[t].at[QB - 1], pools[t].at[EXTRA], extra_send.at[t], extra_recv.at[t], (1, h)
            ).start()

    place_table(rand, me, places)
    back_table(rand, me, returning)
    for t in range(2):
        for b in range(QB):
            pools[t][b] = local[t][b]
        sums[t][...] = jnp.zeros_like(sums[t])
        terms[t][NONE] = jnp.zeros((HD, BLK), bf)
    for copy in loads:
        copy.wait()

    def arrive(t):
        for peer in peers():
            remote(
                packs[t].at[peer], pools[t].at[pl.ds(RECV + peer * SLOTS, SLOTS)],
                ctx_send.at[t, peer], ctx_recv.at[t, peer], (peer, h),
            ).wait_recv()

        @pl.when(me == 1)
        def _():
            remote(
                local[t].at[QB - 1], pools[t].at[EXTRA], extra_send.at[t], extra_recv.at[t], (0, h)
            ).wait_recv()

    def collect(t, i):
        for e in range(ENTRIES):
            listed[e * BLK : (e + 1) * BLK, :] = pools[t][places[i * ENTRIES + e]]

    def rows_of(i, j):
        rows = pl.ds(pl.multiple_of(i * BLK, BLK), BLK)
        return [(rows, slice((j * PER + n) * HD, (j * PER + n + 1) * HD)) for n in range(PER)]

    def stacked(ref, where):
        return jnp.concatenate([ref[w] for w in where], 0)

    def spread(ref, where, value):
        for n, w in enumerate(where):
            ref[w] = value[n * BLK : (n + 1) * BLK].astype(bf)

    def bank(t, i, factor):
        for e in range(ENTRIES):
            term = part[:, e * BLK : (e + 1) * BLK] * factor
            if e < 3:
                sums[t][i + e] += term
            elif e < 3 + GLOB:
                sums[t][QB + 2 + e - 3] += term
            else:
                terms[t][i * RAND + e - 3 - GLOB] = term.astype(bf)

    def give_back(t):
        for n in range(GLOB):
            terms[t][NAMED + n] = sums[t][QB + 2 + n].astype(bf)
        terms[t][EDGE] = sums[t][0].astype(bf)
        terms[t][EDGE + 1] = sums[t][QB + 1].astype(bf)

        @pl.when(me == 0)
        def _():
            for n in range(GLOB):
                sums[t][1 + n] += sums[t][QB + 2 + n]

        for peer in peers():
            for k in range(SLOTS):
                backs[t][peer, k] = terms[t][returning[peer * 2 + k]]
        for peer in peers():
            sent.append(
                remote(
                    backs[t].at[peer], arrived[t].at[me],
                    ret_send.at[t, peer], ret_recv.at[t, me], (peer, h),
                )
            )
            sent[-1].start()

        @pl.when(me == 1)
        def _():
            remote(terms[t].at[EDGE], extras[t], extra_send.at[t], extra_recv.at[t], (0, h)).start()

    def finish(t, ref):
        def body(n, carry):
            peer = lax.rem(me + n, CTX)
            remote(
                backs[t].at[peer], arrived[t].at[peer],
                ret_send.at[t, peer], ret_recv.at[t, peer], (peer, h),
            ).wait_recv()
            for k in range(SLOTS):
                place = outgoing[peer * 2 + k]
                term = arrived[t][peer, k].astype(jnp.float32)
                for b in range(QB):
                    sums[t][1 + b] += term * (place == b).astype(jnp.float32)
            return carry

        lax.fori_loop(1, CTX, body, 0)

        @pl.when(me == 0)
        def _():
            remote(terms[t].at[EDGE], extras[t], extra_send.at[t], extra_recv.at[t], (1, h)).wait_recv()
            sums[t][QB] += extras[t][...].astype(jnp.float32)

        for b in range(QB):
            stages[t][b] = sums[t][1 + b].T.astype(bf)
        for _, peer in heads():
            sent.append(
                remote(
                    stages[t].at[peer], ref.at[:, cols(h)],
                    home_send.at[t, peer], home_recv.at[t, h], (me, peer),
                )
            )
            sent[-1].start()
        own.append(pltpu.make_async_copy(stages[t].at[h], ref.at[:, cols(h)], home_own.at[t]))
        own[-1].start()

    arrive(0)

    def weigh(i, carry):
        collect(0, i)
        for j in range(HALVES):
            where = rows_of(i, j)
            s = mm(stacked(q, where), listed[...], NT)
            parts = []
            for e in range(ENTRIES):
                piece = s[:, e * BLK : (e + 1) * BLK]
                if e < 3:
                    gid = me * QB + i - 1 + e
                    ok = (gid >= GLOB) & (gid < NKB)
                    piece = piece + jnp.where(ok, 0.0, MASKED).astype(jnp.float32)
                parts.append(piece)
            s = jnp.concatenate(parts, 1)
            top = jnp.max(s, 1, keepdims=True)
            p = jnp.exp2(s * (SCALE * LOG2E) - top * (SCALE * LOG2E))
            inv = 1.0 / jnp.sum(p, 1, keepdims=True)
            pb = p.astype(bf)
            gb = (stacked(g, where).astype(jnp.float32) * inv).astype(bf)
            probs[i * HALVES + j] = pb
            inverse[i * HALVES + j] = inv
            spread(g, where, gb)
            more = mm(gb, pb, TN)
            part[...] = more if j == 0 else part[...] + more
        bank(1, i, 1.0)
        return carry

    lax.fori_loop(0, QB, weigh, 0)
    give_back(1)
    arrive(1)

    def blame(i, carry):
        collect(1, i)
        for j in range(HALVES):
            where = rows_of(i, j)
            pb = probs[i * HALVES + j]
            gb = stacked(g, where)
            out = mm(pb, listed[...]) * inverse[i * HALVES + j]
            spread(o, where, out)
            centre = jnp.sum(gb.astype(jnp.float32) * out, 1, keepdims=True)
            dp = mm(gb, listed[...], NT)
            ds = (pb.astype(jnp.float32) * (dp - centre)).astype(bf)
            probs[i * HALVES + j] = ds
            more = mm(stacked(q, where), ds, TN)
            part[...] = more if j == 0 else part[...] + more
        bank(0, i, SCALE)
        return carry

    lax.fori_loop(0, QB, blame, 0)
    give_back(0)
    stores = [pltpu.make_async_copy(o, o_hbm, out_sem.at[0])]
    stores[-1].start()
    finish(1, dv_ref)

    def steer(i, carry):
        collect(0, i)
        for j in range(HALVES):
            spread(dq, rows_of(i, j), mm(probs[i * HALVES + j], listed[...]) * SCALE)
        return carry

    lax.fori_loop(0, QB, steer, 0)
    stores.append(pltpu.make_async_copy(dq, dq_hbm, out_sem.at[1]))
    stores[-1].start()
    finish(0, dk_ref)
    for t in range(2):

        @pl.when(me == 0)
        def _():
            remote(
                local[t].at[QB - 1], pools[t].at[EXTRA], extra_send.at[t], extra_recv.at[t], (1, h)
            ).wait_send()

        @pl.when(me == 1)
        def _():
            remote(terms[t].at[EDGE], extras[t], extra_send.at[t], extra_recv.at[t], (0, h)).wait_send()

    for copy in sent:
        copy.wait_send()
    for copy in own[2:] + stores:
        copy.wait()
    for t, ref in ((1, dv_ref), (0, dk_ref)):
        for _, peer in heads():
            remote(
                stages[t].at[peer], ref.at[:, cols(peer)],
                home_send.at[t, peer], home_recv.at[t, peer], (me, peer),
            ).wait_recv()


SM = pl.BlockSpec(memory_space=pltpu.SMEM)
ANY = pl.BlockSpec(memory_space=pl.ANY)
DMA = pltpu.SemaphoreType.DMA
VMEM_BYTES = 60 * 2**20


def per_device(queries, keys, values, out_grad, random_blocks):
    bf = jnp.bfloat16
    f32 = jnp.float32
    tok = QB * BLK
    big = pltpu.VMEM((tok, HEADS * HD), bf)
    slots = pltpu.VMEM((CTX, SLOTS, BLK, HD), bf)
    two = lambda shape, kind: [pltpu.VMEM(shape, kind)] * 2
    wide = jax.ShapeDtypeStruct((tok, HEADS * HD), bf)
    home = jax.ShapeDtypeStruct((BLK, KVH * HD), bf)
    return pl.pallas_call(
        step_kernel,
        out_shape=[wide, wide, home, home],
        in_specs=[SM, ANY, ANY, ANY, ANY],
        out_specs=[ANY] * 4,
        scratch_shapes=[big] * 4
        + [
            pltpu.VMEM((QB * HALVES, CHUNK, ENTRIES * BLK), bf),
            pltpu.VMEM((QB * HALVES, CHUNK, 1), f32),
        ]
        + two((QB, BLK, HD), bf)
        + two((POOL, BLK, HD), bf)
        + [slots] * 6
        + two((NONE + 1, HD, BLK), bf)
        + two((SUMS, HD, BLK), f32)
        + two((QB, BLK, HD), bf)
        + two((HD, BLK), bf)
        + [
            pltpu.VMEM((ENTRIES * BLK, HD), bf),
            pltpu.VMEM((HD, ENTRIES * BLK), f32),
            pltpu.SMEM((CTX * SLOTS,), jnp.int32),
            pltpu.SMEM((CTX * SLOTS,), jnp.int32),
            pltpu.SMEM((QB * ENTRIES,), jnp.int32),
        ]
        + [DMA((2, KVH))] * 2
        + [DMA((2, CTX))] * 2
        + [DMA((2, KVH))] * 2
        + [DMA((2, CTX))] * 2
        + [DMA((2,))] * 6,
        compiler_params=pltpu.CompilerParams(
            collective_id=0, has_side_effects=True, vmem_limit_bytes=VMEM_BYTES
        ),
    )(random_blocks.reshape(-1), queries, out_grad, keys, values)


def solution(mesh):
    in_specs = (
        P("ctx", "kvh"),
        P(("ctx", "kvh"), None),
        P(("ctx", "kvh"), None),
        P("ctx", "kvh"),
        P(),
    )
    out_specs = (P("ctx", "kvh"), P("ctx", "kvh"), P(("ctx", "kvh"), None), P(("ctx", "kvh"), None))
    return jax.shard_map(
        per_device, mesh=mesh, in_specs=in_specs, out_specs=out_specs, check_vma=False
    )
```

```python
import functools

import jax
import jax.numpy as jnp
from jax import lax
from jax.experimental import pallas as pl
from jax.experimental.pallas import tpu as pltpu
from jax.sharding import PartitionSpec as P

HD = 128
BLK = 128
GLOB = 2
RAND = 3
QB = 8
CTX = 16
KVH = 8
HEADS = 8
SLOTS = 2
NKB = QB * CTX
SIDE = 4
EXTRA = QB
RECV = QB + 1
POOL = RECV + CTX * SLOTS
ENTRIES = 3 + GLOB + RAND
CHUNK = 256
PER = CHUNK // BLK
UNITS = HEADS // PER
PAIR = 2 * PER
HALF = 2 * CHUNK
NAMED = QB * RAND
EDGE = NAMED + GLOB
NONE = EDGE + 2
SUMS = QB + 2 + GLOB
SCALE = HD**-0.5
LOG2E = 1.4426950408889634
MASKED = 1e30
MESH = pl.DeviceIdType.MESH
ORDER = (
    (0, 1), (1, 0), (0, 3), (3, 0), (1, 1), (2, 0), (3, 3), (0, 2),
    (1, 3), (2, 1), (3, 1), (1, 2), (2, 3), (3, 2), (2, 2),
)

NT = (((1,), (1,)), ((), ()))
TN = (((0,), (0,)), ((), ()))


def mm(a, b, dims=(((1,), (0,)), ((), ()))):
    return lax.dot_general(a, b, dims, preferred_element_type=jnp.float32)


def ctx_at(me, dz, dx):
    return lax.rem(me // SIDE + dz, SIDE) * SIDE + lax.rem(me % SIDE + dx, SIDE)


def pick(rand, row, owner, name):
    first = second = jnp.int32(name(None, None))
    count = jnp.int32(0)
    for n in range(NAMED):
        r = rand[n % RAND, row * QB + n // RAND]
        hit = (r >> 3) == owner
        first = jnp.where(hit & (count == 0), name(r, n), first)
        second = jnp.where(hit & (count == 1), name(r, n), second)
        count = count + hit.astype(jnp.int32)
    return first, second


def send_table(rand, me, table):
    def body(dest, carry):
        first, second = pick(rand, dest, me, lambda r, n: 0 if r is None else r & 7)
        first = jnp.where(dest == me + 1, QB - 1, first)
        table[dest * 2] = jnp.where(me == 0, 0, first)
        table[dest * 2 + 1] = jnp.where(me == 0, 1, second)
        return carry

    lax.fori_loop(0, CTX, body, 0)


def back_table(rand, me, table):
    def body(src, carry):
        first, second = pick(rand, me, src, lambda r, n: NONE if r is None else n)
        first = jnp.where(src == me - 1, EDGE, first)
        first = jnp.where(src == me + 1, EDGE + 1, first)
        table[src * 2] = jnp.where(src == 0, NAMED, first)
        table[src * 2 + 1] = jnp.where(src == 0, NAMED + 1, second)
        return carry

    lax.fori_loop(0, CTX, body, 0)


def place_table(rand, me, table):
    def body(i, carry):
        for e in range(3):
            gid = me * QB + i - 1 + e
            near = i - 1 + e
            before = jnp.where(me == 1, EXTRA, RECV + (me - 1) * SLOTS)
            after = RECV + (me + 1) * SLOTS
            place = jnp.where(near < 0, before, jnp.where(near >= QB, after, near))
            ok = (gid >= GLOB) & (gid < NKB)
            table[i * ENTRIES + e] = jnp.where(ok, place, jnp.where(me == 0, 0, RECV))
        for e in range(GLOB):
            table[i * ENTRIES + 3 + e] = jnp.where(me == 0, e, RECV + e)
        for e in range(RAND):
            owner = rand[e, me * QB + i] >> 3
            rank = jnp.int32(0)
            for n in range(NAMED):
                same = ((rand[n % RAND, me * QB + n // RAND] >> 3) == owner) & (n < i * RAND + e)
                rank = rank + same.astype(jnp.int32)
            table[i * ENTRIES + 3 + GLOB + e] = RECV + owner * SLOTS + rank
        return carry

    lax.fori_loop(0, QB, body, 0)


def greet(me, h):
    barrier = pltpu.get_barrier_semaphore()
    for dz, dx in ORDER:
        peer = (ctx_at(me, dz, dx), h)
        pl.semaphore_signal(barrier, inc=1, device_id=peer, device_id_type=MESH)
    for dh in range(1, KVH):
        peer = (me, lax.rem(h + dh, KVH))
        pl.semaphore_signal(barrier, inc=1, device_id=peer, device_id_type=MESH)
    pl.semaphore_wait(barrier, CTX + KVH - 2)


def remote(src, dst, send, recv, peer):
    return pltpu.make_async_remote_copy(
        src_ref=src, dst_ref=dst, send_sem=send, recv_sem=recv, device_id=peer, device_id_type=MESH
    )


def step_kernel(
    rand, q_hbm, g_hbm, key_ref, value_ref,
    o_hbm, dq_hbm, dk_ref, dv_ref,
    q, g, o, dq, probs, inverse, left, right, out_left, out_right, heads_k, heads_v, local_k, local_v, pool_k, pool_v, packed_k, packed_v, back_k, back_v,
    arrived_k, arrived_v, terms_k, terms_v, sums_k, sums_v, stage_k, stage_v, extra_k, extra_v,
    listed, part, outgoing, returning, places,
    head_send, head_recv, ctx_send, ctx_recv, home_send, home_recv, ret_send, ret_recv,
    extra_send, extra_recv, own_sem, home_own, in_sem, out_sem, stage_sem,
):
    me = lax.axis_index("ctx")
    h = lax.axis_index("kvh")
    bf = jnp.bfloat16
    pools, packs, backs = (pool_k, pool_v), (packed_k, packed_v), (back_k, back_v)
    local = (local_k, local_v)
    arrived, terms, sums = (arrived_k, arrived_v), (terms_k, terms_v), (sums_k, sums_v)
    stages, extras = (stage_k, stage_v), (extra_k, extra_v)
    loads = [
        pltpu.make_async_copy(q_hbm, q, in_sem.at[0]),
        pltpu.make_async_copy(g_hbm, g, in_sem.at[1]),
    ]
    for copy in loads:
        copy.start()
    heads_in = (heads_k, heads_v)
    for t, ref in enumerate((key_ref, value_ref)):
        for head in range(KVH):
            loads.append(
                pltpu.make_async_copy(
                    ref.at[:, head * HD : (head + 1) * HD], heads_in[t].at[head], stage_sem.at[t, head]
                )
            )
            loads[-1].start()
    greet(me, h)
    cols = lambda head: pl.ds(pl.multiple_of(head * HD, HD), HD)
    heads = lambda: [(dh, lax.rem(h + dh, KVH)) for dh in range(1, KVH)]
    peers = lambda: [ctx_at(me, dz, dx) for dz, dx in ORDER]
    sent = []
    own = []
    for t in range(2):
        for head in range(KVH):
            loads[2 + t * KVH + head].wait()
        for _, peer in heads():
            sent.append(
                remote(
                    heads_in[t].at[peer], local[t].at[h],
                    head_send.at[t, peer], head_recv.at[t, h], (me, peer),
                )
            )
            sent[-1].start()
        own.append(pltpu.make_async_copy(heads_in[t].at[h], local[t].at[h], own_sem.at[t]))
        own[-1].start()
    send_table(rand, me, outgoing)
    for t in range(2):
        own[t].wait()
        for _, peer in heads():
            remote(
                local[t].at[peer], local[t].at[peer],
                head_send.at[t, peer], head_recv.at[t, peer], (me, peer),
            ).wait_recv()
        for peer in peers():
            for k in range(SLOTS):
                packs[t][peer, k] = local[t][outgoing[peer * 2 + k]]
        for peer in peers():
            sent.append(
                remote(
                    packs[t].at[peer], pools[t].at[pl.ds(RECV + me * SLOTS, SLOTS)],
                    ctx_send.at[t, peer], ctx_recv.at[t, me], (peer, h),
                )
            )
            sent[-1].start()

        @pl.when(me == 0)
        def _():
            remote(
                local[t].at[QB - 1], pools[t].at[EXTRA], extra_send.at[t], extra_recv.at[t], (1, h)
            ).start()

    place_table(rand, me, places)
    back_table(rand, me, returning)
    for t in range(2):
        for b in range(QB):
            pools[t][b] = local[t][b]
        sums[t][...] = jnp.zeros_like(sums[t])
        terms[t][NONE] = jnp.zeros((HD, BLK), bf)
    for copy in loads[:2]:
        copy.wait()

    def arrive(t):
        for peer in peers():
            remote(
                packs[t].at[peer], pools[t].at[pl.ds(RECV + peer * SLOTS, SLOTS)],
                ctx_send.at[t, peer], ctx_recv.at[t, peer], (peer, h),
            ).wait_recv()

        @pl.when(me == 1)
        def _():
            remote(
                local[t].at[QB - 1], pools[t].at[EXTRA], extra_send.at[t], extra_recv.at[t], (0, h)
            ).wait_recv()

    def collect(t, i):
        for e in range(ENTRIES):
            listed[e * BLK : (e + 1) * BLK, :] = pools[t][places[i * ENTRIES + e]]

    def rows_of(i, first, count):
        rows = pl.ds(pl.multiple_of(i * BLK, BLK), BLK)
        return [(rows, slice(n * HD, (n + 1) * HD)) for n in range(first, first + count)]

    def unit(i, u):
        return rows_of(i, u * PER, PER), slice(u * CHUNK, (u + 1) * CHUNK)

    def fold(u, term):
        part[...] = term if u == 1 else part[...] + term

    def stacked(ref, where):
        return jnp.concatenate([ref[w] for w in where], 0)

    def spread(ref, where, value):
        for n, w in enumerate(where):
            ref[w] = value[n * BLK : (n + 1) * BLK].astype(bf)

    def bank(t, i, factor):
        for e in range(ENTRIES):
            term = part[:, e * BLK : (e + 1) * BLK] * factor
            if e < 3:
                sums[t][i + e] += term
            elif e < 3 + GLOB:
                sums[t][QB + 2 + e - 3] += term
            else:
                terms[t][i * RAND + e - 3 - GLOB] = term.astype(bf)

    def give_back(t):
        for n in range(GLOB):
            terms[t][NAMED + n] = sums[t][QB + 2 + n].astype(bf)
        terms[t][EDGE] = sums[t][0].astype(bf)
        terms[t][EDGE + 1] = sums[t][QB + 1].astype(bf)

        @pl.when(me == 0)
        def _():
            for n in range(GLOB):
                sums[t][1 + n] += sums[t][QB + 2 + n]

        for peer in peers():
            for k in range(SLOTS):
                backs[t][peer, k] = terms[t][returning[peer * 2 + k]]
        for peer in peers():
            sent.append(
                remote(
                    backs[t].at[peer], arrived[t].at[me],
                    ret_send.at[t, peer], ret_recv.at[t, me], (peer, h),
                )
            )
            sent[-1].start()

        @pl.when(me == 1)
        def _():
            remote(terms[t].at[EDGE], extras[t], extra_send.at[t], extra_recv.at[t], (0, h)).start()

    def finish(t, ref):
        for dz, dx in ORDER:
            peer = ctx_at(me, SIDE - dz, SIDE - dx)
            remote(
                backs[t].at[peer], arrived[t].at[peer],
                ret_send.at[t, peer], ret_recv.at[t, peer], (peer, h),
            ).wait_recv()
            first = arrived[t][peer, 0].astype(jnp.float32)
            second = arrived[t][peer, 1].astype(jnp.float32)
            for b in range(QB):
                sums[t][1 + b] += first * (outgoing[peer * 2] == b).astype(jnp.float32) + second * (
                    outgoing[peer * 2 + 1] == b
                ).astype(jnp.float32)

        @pl.when(me == 0)
        def _():
            remote(terms[t].at[EDGE], extras[t], extra_send.at[t], extra_recv.at[t], (1, h)).wait_recv()
            sums[t][QB] += extras[t][...].astype(jnp.float32)

        for b in range(QB):
            stages[t][b] = sums[t][1 + b].T.astype(bf)
        for _, peer in heads():
            sent.append(
                remote(
                    stages[t].at[peer], ref.at[:, cols(h)],
                    home_send.at[t, peer], home_recv.at[t, h], (me, peer),
                )
            )
            sent[-1].start()
        own.append(pltpu.make_async_copy(stages[t].at[h], ref.at[:, cols(h)], home_own.at[t]))
        own[-1].start()

    arrive(0)

    def score(i, u, buf):
        where = rows_of(i, u * PAIR, PAIR)
        buf[...] = mm(stacked(q, where), listed[...], NT)

    def soften(i, u, buf):
        where = rows_of(i, u * PAIR, PAIR)
        span = slice(u * HALF, (u + 1) * HALF)
        s = buf[...]
        top = jnp.max(s, 1, keepdims=True) * (SCALE * LOG2E)
        parts = []
        for e in range(ENTRIES):
            gid = me * QB + i - 1 + e
            ok = (gid >= GLOB) & (gid < NKB)
            base = top + jnp.where(ok, 0.0, MASKED).astype(jnp.float32) if e < 3 else top
            parts.append(jnp.exp2(s[:, e * BLK : (e + 1) * BLK] * (SCALE * LOG2E) - base))
        p = jnp.concatenate(parts, 1)
        inv = 1.0 / jnp.sum(p, 1, keepdims=True)
        probs[i, span] = p.astype(bf)
        inverse[i, span] = inv
        spread(g, where, stacked(g, where).astype(jnp.float32) * inv)

    def both(ref, i, u):
        return stacked(ref, rows_of(i, (u - 1) * PER, 2 * PER))

    def weigh(i, carry):
        following = jnp.minimum(i + 1, QB - 1)
        score(i, 1, right)
        soften(i, 0, left)
        collect(0, following)
        score(following, 0, left)
        soften(i, 1, right)
        part[...] = mm(stacked(g, rows_of(i, 0, HEADS)), probs[i], TN)
        bank(1, i, 1.0)
        return carry

    collect(0, 0)
    score(0, 0, left)
    lax.fori_loop(0, QB, weigh, 0)
    give_back(1)
    arrive(1)

    def project(i, u, buf, out):
        where, span = unit(i, u)
        out[...] = mm(probs[i, span], listed[...])
        buf[:CHUNK] = mm(stacked(g, where), listed[...], NT)

    def grade(i, u, buf, out):
        where, span = unit(i, u)
        value = out[...] * inverse[i, span]
        spread(o, where, value)
        centre = jnp.sum(stacked(g, where).astype(jnp.float32) * value, 1, keepdims=True)
        probs[i, span] = (probs[i, span].astype(jnp.float32) * (buf[:CHUNK] - centre)).astype(bf)

    def blame(i, carry):
        for u in range(UNITS):
            here, there = (left, right) if u % 2 == 0 else (right, left)
            out, ahead = (out_left, out_right) if u % 2 == 0 else (out_right, out_left)
            if u + 1 < UNITS:
                project(i, u + 1, there, ahead)
            else:
                following = jnp.minimum(i + 1, QB - 1)
                collect(1, following)
                project(following, 0, there, ahead)
            grade(i, u, here, out)
            if u % 2 == 1:
                fold(u, mm(both(q, i, u), probs[i, (u - 1) * CHUNK : (u + 1) * CHUNK], TN))
        bank(0, i, SCALE)
        return carry

    collect(1, 0)
    project(0, 0, left, out_left)
    lax.fori_loop(0, QB, blame, 0)
    give_back(0)
    stores = [pltpu.make_async_copy(o, o_hbm, out_sem.at[0])]
    stores[-1].start()
    finish(1, dv_ref)

    def steer(i, carry):
        collect(0, i)
        for u in range(1, UNITS, 2):
            where = rows_of(i, (u - 1) * PER, 2 * PER)
            spread(dq, where, mm(probs[i, (u - 1) * CHUNK : (u + 1) * CHUNK], listed[...]) * SCALE)
        return carry

    lax.fori_loop(0, QB, steer, 0)
    stores.append(pltpu.make_async_copy(dq, dq_hbm, out_sem.at[1]))
    stores[-1].start()
    finish(0, dk_ref)
    for t in range(2):

        @pl.when(me == 0)
        def _():
            remote(
                local[t].at[QB - 1], pools[t].at[EXTRA], extra_send.at[t], extra_recv.at[t], (1, h)
            ).wait_send()

        @pl.when(me == 1)
        def _():
            remote(terms[t].at[EDGE], extras[t], extra_send.at[t], extra_recv.at[t], (0, h)).wait_send()

    for copy in sent:
        copy.wait_send()
    for copy in own[2:] + stores:
        copy.wait()
    for t, ref in ((1, dv_ref), (0, dk_ref)):
        for _, peer in heads():
            remote(
                stages[t].at[peer], ref.at[:, cols(peer)],
                home_send.at[t, peer], home_recv.at[t, peer], (me, peer),
            ).wait_recv()


def copy_kernel(*refs):
    count = len(refs) // 3
    ins, outs, held = refs[:count], refs[count : 2 * count], refs[2 * count : 3 * count]
    read_sem, write_sem = refs[3 * count :]
    steps = []
    for n in range(count):
        rows = ins[n].shape[0]
        size = min(rows, 2 * BLK)
        for start in range(0, rows, size):
            steps.append((n, slice(start, start + size)))
    reads = [
        pltpu.make_async_copy(ins[n].at[rows], held[n].at[rows], read_sem.at[i])
        for i, (n, rows) in enumerate(steps)
    ]
    writes = [
        pltpu.make_async_copy(held[n].at[rows], outs[n].at[rows], write_sem.at[i])
        for i, (n, rows) in enumerate(steps)
    ]
    for copy in reads:
        copy.start()
    for read, write in zip(reads, writes):
        read.wait()
        write.start()
    for copy in writes:
        copy.wait()


SM = pl.BlockSpec(memory_space=pltpu.SMEM)
ANY = pl.BlockSpec(memory_space=pl.ANY)
DMA = pltpu.SemaphoreType.DMA
VMEM_BYTES = 60 * 2**20


def per_device(queries, keys, values, out_grad, random_blocks):
    bf = jnp.bfloat16
    f32 = jnp.float32
    tok = QB * BLK
    big = pltpu.VMEM((tok, HEADS * HD), bf)
    slots = pltpu.VMEM((CTX, SLOTS, BLK, HD), bf)
    two = lambda shape, kind: [pltpu.VMEM(shape, kind)] * 2
    wide = jax.ShapeDtypeStruct((tok, HEADS * HD), bf)
    home = jax.ShapeDtypeStruct((BLK, KVH * HD), bf)
    results = pl.pallas_call(
        step_kernel,
        out_shape=[wide, wide, home, home],
        in_specs=[SM, ANY, ANY, ANY, ANY],
        out_specs=[ANY] * 4,
        scratch_shapes=[big] * 4
        + [
            pltpu.VMEM((QB, HEADS * BLK, ENTRIES * BLK), bf),
            pltpu.VMEM((QB, HEADS * BLK, 1), f32),
        ]
        + two((HALF, ENTRIES * BLK), f32)
        + two((CHUNK, HD), f32)
        + two((KVH, BLK, HD), bf)
        + two((QB, BLK, HD), bf)
        + two((POOL, BLK, HD), bf)
        + [slots] * 6
        + two((NONE + 1, HD, BLK), bf)
        + two((SUMS, HD, BLK), f32)
        + two((QB, BLK, HD), bf)
        + two((HD, BLK), bf)
        + [
            pltpu.VMEM((ENTRIES * BLK, HD), bf),
            pltpu.VMEM((HD, ENTRIES * BLK), f32),
            pltpu.SMEM((CTX * SLOTS,), jnp.int32),
            pltpu.SMEM((CTX * SLOTS,), jnp.int32),
            pltpu.SMEM((QB * ENTRIES,), jnp.int32),
        ]
        + [DMA((2, KVH))] * 2
        + [DMA((2, CTX))] * 2
        + [DMA((2, KVH))] * 2
        + [DMA((2, CTX))] * 2
        + [DMA((2,))] * 6
        + [DMA((2, KVH))],
        compiler_params=pltpu.CompilerParams(
            collective_id=0, has_side_effects=True, vmem_limit_bytes=VMEM_BYTES
        ),
    )(random_blocks.T, queries, out_grad, keys, values)
    return pl.pallas_call(
        copy_kernel,
        out_shape=[wide, wide, home, home],
        in_specs=[ANY] * 4,
        out_specs=[ANY] * 4,
        scratch_shapes=[big] * 2 + two((BLK, KVH * HD), bf) + [DMA((10,))] * 2,
        compiler_params=pltpu.CompilerParams(vmem_limit_bytes=VMEM_BYTES),
    )(*results)


def solution(mesh):
    in_specs = (
        P("ctx", "kvh"),
        P(("ctx", "kvh"), None),
        P(("ctx", "kvh"), None),
        P("ctx", "kvh"),
        P(),
    )
    out_specs = (P("ctx", "kvh"), P("ctx", "kvh"), P(("ctx", "kvh"), None), P(("ctx", "kvh"), None))
    return jax.shard_map(
        per_device, mesh=mesh, in_specs=in_specs, out_specs=out_specs, check_vma=False
    )
```

```python
import functools

import jax
import jax.numpy as jnp
from jax import lax
from jax.experimental import pallas as pl
from jax.experimental.pallas import tpu as pltpu
from jax.sharding import PartitionSpec as P

HD = 128
BLK = 128
GLOB = 2
RAND = 3
QB = 8
CTX = 16
KVH = 8
HEADS = 8
SLOTS = 2
NKB = QB * CTX
LAG = 4
SIDE = 4
EXTRA = QB
RECV = QB + 1
POOL = RECV + CTX * SLOTS
ENTRIES = 3 + GLOB + RAND
CHUNK = 256
PER = CHUNK // BLK
UNITS = HEADS // PER
PAIR = 2 * PER
HALF = 2 * CHUNK
NAMED = QB * RAND
EDGE = NAMED + GLOB
NONE = EDGE + 2
SUMS = QB + 2 + GLOB
SCALE = HD**-0.5
LOG2E = 1.4426950408889634
MASKED = 1e30
MESH = pl.DeviceIdType.MESH
ORDER = (
    (0, 1), (1, 0), (0, 3), (3, 0), (1, 1), (2, 0), (3, 3), (0, 2),
    (1, 3), (2, 1), (3, 1), (1, 2), (2, 3), (3, 2), (2, 2),
)

NT = (((1,), (1,)), ((), ()))
TN = (((0,), (0,)), ((), ()))


def mm(a, b, dims=(((1,), (0,)), ((), ()))):
    return lax.dot_general(a, b, dims, preferred_element_type=jnp.float32)


def ctx_at(me, dz, dx):
    return lax.rem(me // SIDE + dz, SIDE) * SIDE + lax.rem(me % SIDE + dx, SIDE)


def pick(rand, row, owner, name):
    first = second = jnp.int32(name(None, None))
    count = jnp.int32(0)
    for n in range(NAMED):
        r = rand[n % RAND, row * QB + n // RAND]
        hit = (r >> 3) == owner
        first = jnp.where(hit & (count == 0), name(r, n), first)
        second = jnp.where(hit & (count == 1), name(r, n), second)
        count = count + hit.astype(jnp.int32)
    return first, second


def send_table(rand, me, table):
    def body(dest, carry):
        first, second = pick(rand, dest, me, lambda r, n: 0 if r is None else r & 7)
        first = jnp.where(dest == me + 1, QB - 1, first)
        table[dest * 2] = jnp.where(me == 0, 0, first)
        table[dest * 2 + 1] = jnp.where(me == 0, 1, second)
        return carry

    lax.fori_loop(0, CTX, body, 0)


def back_table(rand, me, table):
    def body(src, carry):
        first, second = pick(rand, me, src, lambda r, n: NONE if r is None else n)
        first = jnp.where(src == me - 1, EDGE, first)
        first = jnp.where(src == me + 1, EDGE + 1, first)
        table[src * 2] = jnp.where(src == 0, NAMED, first)
        table[src * 2 + 1] = jnp.where(src == 0, NAMED + 1, second)
        return carry

    lax.fori_loop(0, CTX, body, 0)


def place_table(rand, me, table):
    def body(i, carry):
        for e in range(3):
            gid = me * QB + i - 1 + e
            near = i - 1 + e
            before = jnp.where(me == 1, EXTRA, RECV + (me - 1) * SLOTS)
            after = RECV + (me + 1) * SLOTS
            place = jnp.where(near < 0, before, jnp.where(near >= QB, after, near))
            ok = (gid >= GLOB) & (gid < NKB)
            table[i * ENTRIES + e] = jnp.where(ok, place, jnp.where(me == 0, 0, RECV))
        for e in range(GLOB):
            table[i * ENTRIES + 3 + e] = jnp.where(me == 0, e, RECV + e)
        for e in range(RAND):
            owner = rand[e, me * QB + i] >> 3
            rank = jnp.int32(0)
            for n in range(NAMED):
                same = ((rand[n % RAND, me * QB + n // RAND] >> 3) == owner) & (n < i * RAND + e)
                rank = rank + same.astype(jnp.int32)
            table[i * ENTRIES + 3 + GLOB + e] = RECV + owner * SLOTS + rank
        return carry

    lax.fori_loop(0, QB, body, 0)


def greet(me, h):
    barrier = pltpu.get_barrier_semaphore()
    for dz, dx in ORDER:
        peer = (ctx_at(me, dz, dx), h)
        pl.semaphore_signal(barrier, inc=1, device_id=peer, device_id_type=MESH)
    for dh in range(1, KVH):
        peer = (me, lax.rem(h + dh, KVH))
        pl.semaphore_signal(barrier, inc=1, device_id=peer, device_id_type=MESH)
    pl.semaphore_wait(barrier, CTX + KVH - 2)


def remote(src, dst, send, recv, peer):
    return pltpu.make_async_remote_copy(
        src_ref=src, dst_ref=dst, send_sem=send, recv_sem=recv, device_id=peer, device_id_type=MESH
    )


def step_kernel(
    rand, q_hbm, g_hbm, key_ref, value_ref,
    o, dq, dk_ref, dv_ref,
    q, g, probs, inverse, left, right, out_left, out_right, heads_k, heads_v, local_k, local_v, pool_k, pool_v, packed_k, packed_v, back_k, back_v,
    arrived_k, arrived_v, terms_k, terms_v, sums_k, sums_v, stage_k, stage_v, extra_k, extra_v,
    listed, part, outgoing, returning, places,
    head_send, head_recv, ctx_send, ctx_recv, home_send, home_recv, ret_send, ret_recv,
    extra_send, extra_recv, own_sem, home_own, in_sem, stage_sem,
):
    me = lax.axis_index("ctx")
    h = lax.axis_index("kvh")
    bf = jnp.bfloat16
    pools, packs, backs = (pool_k, pool_v), (packed_k, packed_v), (back_k, back_v)
    local = (local_k, local_v)
    arrived, terms, sums = (arrived_k, arrived_v), (terms_k, terms_v), (sums_k, sums_v)
    stages, extras = (stage_k, stage_v), (extra_k, extra_v)
    loads = [
        pltpu.make_async_copy(q_hbm, q, in_sem.at[0]),
        pltpu.make_async_copy(g_hbm, g, in_sem.at[1]),
    ]
    for copy in loads:
        copy.start()
    heads_in = (heads_k, heads_v)
    for t, ref in enumerate((key_ref, value_ref)):
        for head in range(KVH):
            loads.append(
                pltpu.make_async_copy(
                    ref.at[:, head * HD : (head + 1) * HD], heads_in[t].at[head], stage_sem.at[t, head]
                )
            )
            loads[-1].start()
    greet(me, h)
    cols = lambda head: pl.ds(pl.multiple_of(head * HD, HD), HD)
    heads = lambda: [(dh, lax.rem(h + dh, KVH)) for dh in range(1, KVH)]
    peers = lambda: [ctx_at(me, dz, dx) for dz, dx in ORDER]
    sent = []
    own = []

    def trail(pack, push):
        order = peers()
        for n in range(len(order) + LAG):
            if n < len(order):
                pack(order[n])
            if n >= LAG:
                push(order[n - LAG])

    for t in range(2):
        for head in range(KVH):
            loads[2 + t * KVH + head].wait()
        for _, peer in heads():
            sent.append(
                remote(
                    heads_in[t].at[peer], local[t].at[h],
                    head_send.at[t, peer], head_recv.at[t, h], (me, peer),
                )
            )
            sent[-1].start()
        own.append(pltpu.make_async_copy(heads_in[t].at[h], local[t].at[h], own_sem.at[t]))
        own[-1].start()
    send_table(rand, me, outgoing)
    for t in range(2):
        own[t].wait()
        for _, peer in heads():
            remote(
                local[t].at[peer], local[t].at[peer],
                head_send.at[t, peer], head_recv.at[t, peer], (me, peer),
            ).wait_recv()

        def pack(peer):
            for k in range(SLOTS):
                packs[t][peer, k] = local[t][outgoing[peer * 2 + k]]

        def push(peer):
            sent.append(
                remote(
                    packs[t].at[peer], pools[t].at[pl.ds(RECV + me * SLOTS, SLOTS)],
                    ctx_send.at[t, peer], ctx_recv.at[t, me], (peer, h),
                )
            )
            sent[-1].start()

        trail(pack, push)

        @pl.when(me == 0)
        def _():
            remote(
                local[t].at[QB - 1], pools[t].at[EXTRA], extra_send.at[t], extra_recv.at[t], (1, h)
            ).start()

    place_table(rand, me, places)
    back_table(rand, me, returning)
    for t in range(2):
        for b in range(QB):
            pools[t][b] = local[t][b]
        sums[t][...] = jnp.zeros_like(sums[t])
        terms[t][NONE] = jnp.zeros((HD, BLK), bf)
    for copy in loads[:2]:
        copy.wait()

    def arrive(t):
        for peer in peers():
            remote(
                packs[t].at[peer], pools[t].at[pl.ds(RECV + peer * SLOTS, SLOTS)],
                ctx_send.at[t, peer], ctx_recv.at[t, peer], (peer, h),
            ).wait_recv()

        @pl.when(me == 1)
        def _():
            remote(
                local[t].at[QB - 1], pools[t].at[EXTRA], extra_send.at[t], extra_recv.at[t], (0, h)
            ).wait_recv()

    def collect(t, i):
        for e in range(ENTRIES):
            listed[e * BLK : (e + 1) * BLK, :] = pools[t][places[i * ENTRIES + e]]

    def rows_of(i, first, count):
        rows = pl.ds(pl.multiple_of(i * BLK, BLK), BLK)
        return [(rows, slice(n * HD, (n + 1) * HD)) for n in range(first, first + count)]

    def unit(i, u):
        return rows_of(i, u * PER, PER), slice(u * CHUNK, (u + 1) * CHUNK)

    def fold(u, term):
        part[...] = term if u == 1 else part[...] + term

    def stacked(ref, where):
        return jnp.concatenate([ref[w] for w in where], 0)

    def spread(ref, where, value):
        for n, w in enumerate(where):
            ref[w] = value[n * BLK : (n + 1) * BLK].astype(bf)

    def bank(t, i, factor):
        for e in range(ENTRIES):
            term = part[:, e * BLK : (e + 1) * BLK] * factor
            if e < 3:
                sums[t][i + e] += term
            elif e < 3 + GLOB:
                sums[t][QB + 2 + e - 3] += term
            else:
                terms[t][i * RAND + e - 3 - GLOB] = term.astype(bf)

    def give_back(t):
        for n in range(GLOB):
            terms[t][NAMED + n] = sums[t][QB + 2 + n].astype(bf)
        terms[t][EDGE] = sums[t][0].astype(bf)
        terms[t][EDGE + 1] = sums[t][QB + 1].astype(bf)

        @pl.when(me == 0)
        def _():
            for n in range(GLOB):
                sums[t][1 + n] += sums[t][QB + 2 + n]

        def pack(peer):
            for k in range(SLOTS):
                backs[t][peer, k] = terms[t][returning[peer * 2 + k]]

        def push(peer):
            sent.append(
                remote(
                    backs[t].at[peer], arrived[t].at[me],
                    ret_send.at[t, peer], ret_recv.at[t, me], (peer, h),
                )
            )
            sent[-1].start()

        trail(pack, push)

        @pl.when(me == 1)
        def _():
            remote(terms[t].at[EDGE], extras[t], extra_send.at[t], extra_recv.at[t], (0, h)).start()

    def finish(t, ref):
        for dz, dx in ORDER:
            peer = ctx_at(me, SIDE - dz, SIDE - dx)
            remote(
                backs[t].at[peer], arrived[t].at[peer],
                ret_send.at[t, peer], ret_recv.at[t, peer], (peer, h),
            ).wait_recv()
            first = arrived[t][peer, 0].astype(jnp.float32)
            second = arrived[t][peer, 1].astype(jnp.float32)
            for b in range(QB):
                sums[t][1 + b] += first * (outgoing[peer * 2] == b).astype(jnp.float32) + second * (
                    outgoing[peer * 2 + 1] == b
                ).astype(jnp.float32)

        @pl.when(me == 0)
        def _():
            remote(terms[t].at[EDGE], extras[t], extra_send.at[t], extra_recv.at[t], (1, h)).wait_recv()
            sums[t][QB] += extras[t][...].astype(jnp.float32)

        for b in range(QB):
            stages[t][b] = sums[t][1 + b].T.astype(bf)
        for _, peer in heads():
            sent.append(
                remote(
                    stages[t].at[peer], ref.at[:, cols(h)],
                    home_send.at[t, peer], home_recv.at[t, h], (me, peer),
                )
            )
            sent[-1].start()
        own.append(pltpu.make_async_copy(stages[t].at[h], ref.at[:, cols(h)], home_own.at[t]))
        own[-1].start()

    arrive(0)

    def score(i, u, buf):
        where = rows_of(i, u * PAIR, PAIR)
        buf[...] = mm(stacked(q, where), listed[...], NT)

    def soften(i, u, buf):
        where = rows_of(i, u * PAIR, PAIR)
        span = slice(u * HALF, (u + 1) * HALF)
        s = buf[...]
        top = jnp.max(s, 1, keepdims=True) * (SCALE * LOG2E)
        parts = []
        for e in range(ENTRIES):
            gid = me * QB + i - 1 + e
            ok = (gid >= GLOB) & (gid < NKB)
            base = top + jnp.where(ok, 0.0, MASKED).astype(jnp.float32) if e < 3 else top
            parts.append(jnp.exp2(s[:, e * BLK : (e + 1) * BLK] * (SCALE * LOG2E) - base))
        p = jnp.concatenate(parts, 1)
        inv = 1.0 / jnp.sum(p, 1, keepdims=True)
        probs[i, span] = p.astype(bf)
        inverse[i, span] = inv
        spread(g, where, stacked(g, where).astype(jnp.float32) * inv)

    def both(ref, i, u):
        return stacked(ref, rows_of(i, (u - 1) * PER, 2 * PER))

    def weigh(i, carry):
        following = jnp.minimum(i + 1, QB - 1)
        score(i, 1, right)
        soften(i, 0, left)
        collect(0, following)
        score(following, 0, left)
        soften(i, 1, right)
        part[...] = mm(stacked(g, rows_of(i, 0, HEADS)), probs[i], TN)
        bank(1, i, 1.0)
        return carry

    collect(0, 0)
    score(0, 0, left)
    lax.fori_loop(0, QB, weigh, 0)
    give_back(1)
    arrive(1)

    def project(i, u, buf, out):
        where, span = unit(i, u)
        out[...] = mm(probs[i, span], listed[...])
        buf[:CHUNK] = mm(stacked(g, where), listed[...], NT)

    def grade(i, u, buf, out):
        where, span = unit(i, u)
        value = out[...] * inverse[i, span]
        spread(o, where, value)
        centre = jnp.sum(stacked(g, where).astype(jnp.float32) * value, 1, keepdims=True)
        probs[i, span] = (probs[i, span].astype(jnp.float32) * (buf[:CHUNK] - centre)).astype(bf)

    def blame(i, carry):
        for u in range(UNITS):
            here, there = (left, right) if u % 2 == 0 else (right, left)
            out, ahead = (out_left, out_right) if u % 2 == 0 else (out_right, out_left)
            if u + 1 < UNITS:
                project(i, u + 1, there, ahead)
            else:
                following = jnp.minimum(i + 1, QB - 1)
                collect(1, following)
                project(following, 0, there, ahead)
            grade(i, u, here, out)
            if u % 2 == 1:
                fold(u, mm(both(q, i, u), probs[i, (u - 1) * CHUNK : (u + 1) * CHUNK], TN))
        bank(0, i, SCALE)
        return carry

    collect(1, 0)
    project(0, 0, left, out_left)
    lax.fori_loop(0, QB, blame, 0)
    give_back(0)
    finish(1, dv_ref)

    def steer(i, carry):
        collect(0, i)
        for u in range(1, UNITS, 2):
            where = rows_of(i, (u - 1) * PER, 2 * PER)
            spread(dq, where, mm(probs[i, (u - 1) * CHUNK : (u + 1) * CHUNK], listed[...]) * SCALE)
        return carry

    lax.fori_loop(0, QB, steer, 0)
    finish(0, dk_ref)
    for t in range(2):

        @pl.when(me == 0)
        def _():
            remote(
                local[t].at[QB - 1], pools[t].at[EXTRA], extra_send.at[t], extra_recv.at[t], (1, h)
            ).wait_send()

        @pl.when(me == 1)
        def _():
            remote(terms[t].at[EDGE], extras[t], extra_send.at[t], extra_recv.at[t], (0, h)).wait_send()

    for copy in sent:
        copy.wait_send()
    for copy in own[2:]:
        copy.wait()
    for t, ref in ((1, dv_ref), (0, dk_ref)):
        for _, peer in heads():
            remote(
                stages[t].at[peer], ref.at[:, cols(peer)],
                home_send.at[t, peer], home_recv.at[t, peer], (me, peer),
            ).wait_recv()


def copy_kernel(*refs):
    count = len(refs) // 2
    ins, outs, sem = refs[:count], refs[count : 2 * count], refs[2 * count]
    writes = [
        pltpu.make_async_copy(ins[n], outs[n], sem.at[n]) for n in range(count)
    ]
    for copy in writes:
        copy.start()
    for copy in writes:
        copy.wait()


SM = pl.BlockSpec(memory_space=pltpu.SMEM)
ANY = pl.BlockSpec(memory_space=pl.ANY)
VM = pl.BlockSpec(memory_space=pltpu.VMEM)
DMA = pltpu.SemaphoreType.DMA
VMEM_BYTES = 57 * 2**20


def per_device(queries, keys, values, out_grad, random_blocks):
    bf = jnp.bfloat16
    f32 = jnp.float32
    tok = QB * BLK
    big = pltpu.VMEM((tok, HEADS * HD), bf)
    slots = pltpu.VMEM((CTX, SLOTS, BLK, HD), bf)
    two = lambda shape, kind: [pltpu.VMEM(shape, kind)] * 2
    wide = jax.ShapeDtypeStruct((tok, HEADS * HD), bf)
    home = jax.ShapeDtypeStruct((BLK, KVH * HD), bf)
    results = pl.pallas_call(
        step_kernel,
        out_shape=[big, big, pltpu.VMEM((BLK, KVH * HD), bf), pltpu.VMEM((BLK, KVH * HD), bf)],
        in_specs=[SM, ANY, ANY, ANY, ANY],
        out_specs=[VM] * 4,
        scratch_shapes=[big] * 2
        + [
            pltpu.VMEM((QB, HEADS * BLK, ENTRIES * BLK), bf),
            pltpu.VMEM((QB, HEADS * BLK, 1), f32),
        ]
        + two((HALF, ENTRIES * BLK), f32)
        + two((CHUNK, HD), f32)
        + two((KVH, BLK, HD), bf)
        + two((QB, BLK, HD), bf)
        + two((POOL, BLK, HD), bf)
        + [slots] * 6
        + two((NONE + 1, HD, BLK), bf)
        + two((SUMS, HD, BLK), f32)
        + two((QB, BLK, HD), bf)
        + two((HD, BLK), bf)
        + [
            pltpu.VMEM((ENTRIES * BLK, HD), bf),
            pltpu.VMEM((HD, ENTRIES * BLK), f32),
            pltpu.SMEM((CTX * SLOTS,), jnp.int32),
            pltpu.SMEM((CTX * SLOTS,), jnp.int32),
            pltpu.SMEM((QB * ENTRIES,), jnp.int32),
        ]
        + [DMA((2, KVH))] * 2
        + [DMA((2, CTX))] * 2
        + [DMA((2, KVH))] * 2
        + [DMA((2, CTX))] * 2
        + [DMA((2,))] * 5
        + [DMA((2, KVH))],
        compiler_params=pltpu.CompilerParams(
            collective_id=0, has_side_effects=True, vmem_limit_bytes=VMEM_BYTES
        ),
    )(random_blocks.T, queries, out_grad, keys, values)
    return pl.pallas_call(
        copy_kernel,
        out_shape=[wide, wide, home, home],
        in_specs=[VM] * 4,
        out_specs=[ANY] * 4,
        scratch_shapes=[DMA((4,))],
        compiler_params=pltpu.CompilerParams(vmem_limit_bytes=2**20),
    )(*[pltpu.with_memory_space_constraint(x, pltpu.VMEM) for x in results])


def solution(mesh):
    in_specs = (
        P("ctx", "kvh"),
        P(("ctx", "kvh"), None),
        P(("ctx", "kvh"), None),
        P("ctx", "kvh"),
        P(),
    )
    out_specs = (P("ctx", "kvh"), P("ctx", "kvh"), P(("ctx", "kvh"), None), P(("ctx", "kvh"), None))
    return jax.shard_map(
        per_device, mesh=mesh, in_specs=in_specs, out_specs=out_specs, check_vma=False
    )
```

```python
import functools

import jax
import jax.numpy as jnp
from jax import lax
from jax.experimental import pallas as pl
from jax.experimental.pallas import tpu as pltpu
from jax.sharding import PartitionSpec as P

HD = 128
BLK = 128
GLOB = 2
RAND = 3
QB = 8
CTX = 16
KVH = 8
HEADS = 8
SLOTS = 2
NKB = QB * CTX
LAG = 4
SIDE = 4
EXTRA = QB
RECV = QB + 1
POOL = RECV + CTX * SLOTS
ENTRIES = 3 + GLOB + RAND
CHUNK = 256
PER = CHUNK // BLK
UNITS = HEADS // PER
PAIR = 2 * PER
HALF = 2 * CHUNK
NAMED = QB * RAND
EDGE = NAMED + GLOB
NONE = EDGE + 2
SUMS = QB + 2 + GLOB
SCALE = HD**-0.5
LOG2E = 1.4426950408889634
MASKED = 1e30
MESH = pl.DeviceIdType.MESH
ORDER = (
    (0, 1), (1, 0), (0, 3), (3, 0), (1, 1), (2, 0), (3, 3), (0, 2),
    (1, 3), (2, 1), (3, 1), (1, 2), (2, 3), (3, 2), (2, 2),
)

NT = (((1,), (1,)), ((), ()))
TN = (((0,), (0,)), ((), ()))


def mm(a, b, dims=(((1,), (0,)), ((), ()))):
    return lax.dot_general(a, b, dims, preferred_element_type=jnp.float32)


def ctx_at(me, dz, dx):
    return lax.rem(me // SIDE + dz, SIDE) * SIDE + lax.rem(me % SIDE + dx, SIDE)


def pick(rand, row, owner, name):
    first = second = jnp.int32(name(None, None))
    count = jnp.int32(0)
    for n in range(NAMED):
        r = rand[n % RAND, row * QB + n // RAND]
        hit = (r >> 3) == owner
        first = jnp.where(hit & (count == 0), name(r, n), first)
        second = jnp.where(hit & (count == 1), name(r, n), second)
        count = count + hit.astype(jnp.int32)
    return first, second


def send_table(rand, me, table):
    def body(dest, carry):
        first, second = pick(rand, dest, me, lambda r, n: 0 if r is None else r & 7)
        first = jnp.where(dest == me + 1, QB - 1, first)
        table[dest * 2] = jnp.where(me == 0, 0, first)
        table[dest * 2 + 1] = jnp.where(me == 0, 1, second)
        return carry

    lax.fori_loop(0, CTX, body, 0)


def back_table(rand, me, table):
    def body(src, carry):
        first, second = pick(rand, me, src, lambda r, n: NONE if r is None else n)
        first = jnp.where(src == me - 1, EDGE, first)
        first = jnp.where(src == me + 1, EDGE + 1, first)
        table[src * 2] = jnp.where(src == 0, NAMED, first)
        table[src * 2 + 1] = jnp.where(src == 0, NAMED + 1, second)
        return carry

    lax.fori_loop(0, CTX, body, 0)


def place_table(rand, me, table):
    def body(i, carry):
        for e in range(3):
            gid = me * QB + i - 1 + e
            near = i - 1 + e
            before = jnp.where(me == 1, EXTRA, RECV + (me - 1) * SLOTS)
            after = RECV + (me + 1) * SLOTS
            place = jnp.where(near < 0, before, jnp.where(near >= QB, after, near))
            ok = (gid >= GLOB) & (gid < NKB)
            table[i * ENTRIES + e] = jnp.where(ok, place, jnp.where(me == 0, 0, RECV))
        for e in range(GLOB):
            table[i * ENTRIES + 3 + e] = jnp.where(me == 0, e, RECV + e)
        for e in range(RAND):
            owner = rand[e, me * QB + i] >> 3
            rank = jnp.int32(0)
            for n in range(NAMED):
                same = ((rand[n % RAND, me * QB + n // RAND] >> 3) == owner) & (n < i * RAND + e)
                rank = rank + same.astype(jnp.int32)
            table[i * ENTRIES + 3 + GLOB + e] = RECV + owner * SLOTS + rank
        return carry

    lax.fori_loop(0, QB, body, 0)


def greet(me, h):
    barrier = pltpu.get_barrier_semaphore()
    for dz, dx in reversed(ORDER):
        peer = (ctx_at(me, dz, dx), h)
        pl.semaphore_signal(barrier, inc=1, device_id=peer, device_id_type=MESH)
    for dh in range(1, KVH):
        peer = (me, lax.rem(h + dh, KVH))
        pl.semaphore_signal(barrier, inc=1, device_id=peer, device_id_type=MESH)
    return lambda: pl.semaphore_wait(barrier, CTX + KVH - 2)


def remote(src, dst, send, recv, peer):
    return pltpu.make_async_remote_copy(
        src_ref=src, dst_ref=dst, send_sem=send, recv_sem=recv, device_id=peer, device_id_type=MESH
    )


def step_kernel(
    rand, q_hbm, g_hbm, key_ref, value_ref,
    o, dq, dk_ref, dv_ref,
    q, g, probs, inverse, left, right, out_left, out_right, heads_k, heads_v, local_k, local_v, pool_k, pool_v, packed_k, packed_v, back_k, back_v,
    arrived_k, arrived_v, terms_k, terms_v, sums_k, sums_v, stage_k, stage_v, extra_k, extra_v,
    listed, part, outgoing, returning, places,
    head_send, head_recv, ctx_send, ctx_recv, home_send, home_recv, ret_send, ret_recv,
    extra_send, extra_recv, own_sem, home_own, in_sem, stage_sem,
):
    me = lax.axis_index("ctx")
    h = lax.axis_index("kvh")
    bf = jnp.bfloat16
    pools, packs, backs = (pool_k, pool_v), (packed_k, packed_v), (back_k, back_v)
    local = (local_k, local_v)
    arrived, terms, sums = (arrived_k, arrived_v), (terms_k, terms_v), (sums_k, sums_v)
    stages, extras = (stage_k, stage_v), (extra_k, extra_v)
    met = greet(me, h)
    loads = [
        pltpu.make_async_copy(q_hbm, q, in_sem.at[0]),
        pltpu.make_async_copy(g_hbm, g, in_sem.at[1]),
    ]
    for copy in loads:
        copy.start()
    heads_in = (heads_k, heads_v)
    for t, ref in enumerate((key_ref, value_ref)):
        for head in range(KVH):
            loads.append(
                pltpu.make_async_copy(
                    ref.at[:, head * HD : (head + 1) * HD], heads_in[t].at[head], stage_sem.at[t, head]
                )
            )
            loads[-1].start()
    met()
    cols = lambda head: pl.ds(pl.multiple_of(head * HD, HD), HD)
    heads = lambda: [(dh, lax.rem(h + dh, KVH)) for dh in range(1, KVH)]
    peers = lambda: [ctx_at(me, dz, dx) for dz, dx in ORDER]
    sent = []
    own = []

    def trail(pack, push):
        order = peers()
        for n in range(len(order) + LAG):
            if n < len(order):
                pack(order[n])
            if n >= LAG:
                push(order[n - LAG])

    for t in range(2):
        for head in range(KVH):
            loads[2 + t * KVH + head].wait()
        for _, peer in heads():
            sent.append(
                remote(
                    heads_in[t].at[peer], local[t].at[h],
                    head_send.at[t, peer], head_recv.at[t, h], (me, peer),
                )
            )
            sent[-1].start()
        own.append(pltpu.make_async_copy(heads_in[t].at[h], local[t].at[h], own_sem.at[t]))
        own[-1].start()
    send_table(rand, me, outgoing)
    def forward(t):
        own[t].wait()
        for _, peer in heads():
            remote(
                local[t].at[peer], local[t].at[peer],
                head_send.at[t, peer], head_recv.at[t, peer], (me, peer),
            ).wait_recv()

        def pack(peer):
            for k in range(SLOTS):
                packs[t][peer, k] = local[t][outgoing[peer * 2 + k]]

        def push(peer):
            sent.append(
                remote(
                    packs[t].at[peer], pools[t].at[pl.ds(RECV + me * SLOTS, SLOTS)],
                    ctx_send.at[t, peer], ctx_recv.at[t, me], (peer, h),
                )
            )
            sent[-1].start()

        trail(pack, push)
        for b in range(QB):
            pools[t][b] = local[t][b]

        @pl.when(me == 0)
        def _():
            remote(
                local[t].at[QB - 1], pools[t].at[EXTRA], extra_send.at[t], extra_recv.at[t], (1, h)
            ).start()

    forward(0)
    place_table(rand, me, places)
    back_table(rand, me, returning)
    for t in range(2):
        sums[t][...] = jnp.zeros_like(sums[t])
        terms[t][NONE] = jnp.zeros((HD, BLK), bf)
    for copy in loads[:2]:
        copy.wait()

    def arrive(t):
        for peer in peers():
            remote(
                packs[t].at[peer], pools[t].at[pl.ds(RECV + peer * SLOTS, SLOTS)],
                ctx_send.at[t, peer], ctx_recv.at[t, peer], (peer, h),
            ).wait_recv()

        @pl.when(me == 1)
        def _():
            remote(
                local[t].at[QB - 1], pools[t].at[EXTRA], extra_send.at[t], extra_recv.at[t], (0, h)
            ).wait_recv()

    def collect(t, i):
        for e in range(ENTRIES):
            listed[e * BLK : (e + 1) * BLK, :] = pools[t][places[i * ENTRIES + e]]

    def rows_of(i, first, count):
        rows = pl.ds(pl.multiple_of(i * BLK, BLK), BLK)
        return [(rows, slice(n * HD, (n + 1) * HD)) for n in range(first, first + count)]

    def unit(i, u):
        return rows_of(i, u * PER, PER), slice(u * CHUNK, (u + 1) * CHUNK)

    def fold(u, term):
        part[...] = term if u == 1 else part[...] + term

    def stacked(ref, where):
        return jnp.concatenate([ref[w] for w in where], 0)

    def spread(ref, where, value):
        for n, w in enumerate(where):
            ref[w] = value[n * BLK : (n + 1) * BLK].astype(bf)

    def bank(t, i, factor):
        for e in range(ENTRIES):
            term = part[:, e * BLK : (e + 1) * BLK] * factor
            if e < 3:
                sums[t][i + e] += term
            elif e < 3 + GLOB:
                sums[t][QB + 2 + e - 3] += term
            else:
                terms[t][i * RAND + e - 3 - GLOB] = term.astype(bf)

    def give_back(t):
        for n in range(GLOB):
            terms[t][NAMED + n] = sums[t][QB + 2 + n].astype(bf)
        terms[t][EDGE] = sums[t][0].astype(bf)
        terms[t][EDGE + 1] = sums[t][QB + 1].astype(bf)

        @pl.when(me == 0)
        def _():
            for n in range(GLOB):
                sums[t][1 + n] += sums[t][QB + 2 + n]

        def pack(peer):
            for k in range(SLOTS):
                backs[t][peer, k] = terms[t][returning[peer * 2 + k]]

        def push(peer):
            sent.append(
                remote(
                    backs[t].at[peer], arrived[t].at[me],
                    ret_send.at[t, peer], ret_recv.at[t, me], (peer, h),
                )
            )
            sent[-1].start()

        trail(pack, push)

        @pl.when(me == 1)
        def _():
            remote(terms[t].at[EDGE], extras[t], extra_send.at[t], extra_recv.at[t], (0, h)).start()

    def finish(t, ref):
        for dz, dx in ORDER:
            peer = ctx_at(me, SIDE - dz, SIDE - dx)
            remote(
                backs[t].at[peer], arrived[t].at[peer],
                ret_send.at[t, peer], ret_recv.at[t, peer], (peer, h),
            ).wait_recv()
            first = arrived[t][peer, 0].astype(jnp.float32)
            second = arrived[t][peer, 1].astype(jnp.float32)
            for b in range(QB):
                sums[t][1 + b] += first * (outgoing[peer * 2] == b).astype(jnp.float32) + second * (
                    outgoing[peer * 2 + 1] == b
                ).astype(jnp.float32)

        @pl.when(me == 0)
        def _():
            remote(terms[t].at[EDGE], extras[t], extra_send.at[t], extra_recv.at[t], (1, h)).wait_recv()
            sums[t][QB] += extras[t][...].astype(jnp.float32)

        for b in range(QB):
            stages[t][b] = sums[t][1 + b].T.astype(bf)
        for _, peer in heads():
            sent.append(
                remote(
                    stages[t].at[peer], ref.at[:, cols(h)],
                    home_send.at[t, peer], home_recv.at[t, h], (me, peer),
                )
            )
            sent[-1].start()
        own.append(pltpu.make_async_copy(stages[t].at[h], ref.at[:, cols(h)], home_own.at[t]))
        own[-1].start()

    arrive(0)
    forward(1)

    def score(i, u, buf):
        where = rows_of(i, u * PAIR, PAIR)
        buf[...] = mm(stacked(q, where), listed[...], NT)

    def soften(i, u, buf):
        where = rows_of(i, u * PAIR, PAIR)
        span = slice(u * HALF, (u + 1) * HALF)
        s = buf[...]
        top = jnp.max(s, 1, keepdims=True) * (SCALE * LOG2E)
        parts = []
        for e in range(ENTRIES):
            gid = me * QB + i - 1 + e
            ok = (gid >= GLOB) & (gid < NKB)
            base = top + jnp.where(ok, 0.0, MASKED).astype(jnp.float32) if e < 3 else top
            parts.append(jnp.exp2(s[:, e * BLK : (e + 1) * BLK] * (SCALE * LOG2E) - base))
        p = jnp.concatenate(parts, 1)
        inv = 1.0 / jnp.sum(p, 1, keepdims=True)
        probs[i, span] = p.astype(bf)
        inverse[i, span] = inv
        spread(g, where, stacked(g, where).astype(jnp.float32) * inv)

    def both(ref, i, u):
        return stacked(ref, rows_of(i, (u - 1) * PER, 2 * PER))

    def weigh(i, carry):
        following = jnp.minimum(i + 1, QB - 1)
        score(i, 1, right)
        soften(i, 0, left)
        collect(0, following)
        score(following, 0, left)
        soften(i, 1, right)
        part[...] = mm(stacked(g, rows_of(i, 0, HEADS)), probs[i], TN)
        bank(1, i, 1.0)
        return carry

    collect(0, 0)
    score(0, 0, left)
    lax.fori_loop(0, QB, weigh, 0)
    give_back(1)
    arrive(1)

    def project(i, u, buf, out):
        where, span = unit(i, u)
        out[...] = mm(probs[i, span], listed[...])
        buf[:CHUNK] = mm(stacked(g, where), listed[...], NT)

    def grade(i, u, buf, out):
        where, span = unit(i, u)
        value = out[...] * inverse[i, span]
        spread(o, where, value)
        centre = jnp.sum(stacked(g, where).astype(jnp.float32) * value, 1, keepdims=True)
        probs[i, span] = (probs[i, span].astype(jnp.float32) * (buf[:CHUNK] - centre)).astype(bf)

    def blame(i, carry):
        for u in range(UNITS):
            here, there = (left, right) if u % 2 == 0 else (right, left)
            out, ahead = (out_left, out_right) if u % 2 == 0 else (out_right, out_left)
            if u + 1 < UNITS:
                project(i, u + 1, there, ahead)
            else:
                following = jnp.minimum(i + 1, QB - 1)
                collect(1, following)
                project(following, 0, there, ahead)
            grade(i, u, here, out)
            if u % 2 == 1:
                fold(u, mm(both(q, i, u), probs[i, (u - 1) * CHUNK : (u + 1) * CHUNK], TN))
        bank(0, i, SCALE)
        return carry

    collect(1, 0)
    project(0, 0, left, out_left)
    lax.fori_loop(0, QB, blame, 0)
    give_back(0)
    finish(1, dv_ref)

    def steer(i, carry):
        collect(0, i)
        for u in range(1, UNITS, 2):
            where = rows_of(i, (u - 1) * PER, 2 * PER)
            spread(dq, where, mm(probs[i, (u - 1) * CHUNK : (u + 1) * CHUNK], listed[...]) * SCALE)
        return carry

    lax.fori_loop(0, QB, steer, 0)
    finish(0, dk_ref)
    for t in range(2):

        @pl.when(me == 0)
        def _():
            remote(
                local[t].at[QB - 1], pools[t].at[EXTRA], extra_send.at[t], extra_recv.at[t], (1, h)
            ).wait_send()

        @pl.when(me == 1)
        def _():
            remote(terms[t].at[EDGE], extras[t], extra_send.at[t], extra_recv.at[t], (0, h)).wait_send()

    for copy in sent:
        copy.wait_send()
    for copy in own[2:]:
        copy.wait()
    for t, ref in ((1, dv_ref), (0, dk_ref)):
        for _, peer in heads():
            remote(
                stages[t].at[peer], ref.at[:, cols(peer)],
                home_send.at[t, peer], home_recv.at[t, peer], (me, peer),
            ).wait_recv()


def copy_kernel(*refs):
    count = len(refs) // 2
    ins, outs, sem = refs[:count], refs[count : 2 * count], refs[2 * count]
    writes = [
        pltpu.make_async_copy(ins[n], outs[n], sem.at[n]) for n in range(count)
    ]
    for copy in writes:
        copy.start()
    for copy in writes:
        copy.wait()


SM = pl.BlockSpec(memory_space=pltpu.SMEM)
ANY = pl.BlockSpec(memory_space=pl.ANY)
VM = pl.BlockSpec(memory_space=pltpu.VMEM)
DMA = pltpu.SemaphoreType.DMA
VMEM_BYTES = 57 * 2**20


def per_device(queries, keys, values, out_grad, random_blocks):
    bf = jnp.bfloat16
    f32 = jnp.float32
    tok = QB * BLK
    big = pltpu.VMEM((tok, HEADS * HD), bf)
    slots = pltpu.VMEM((CTX, SLOTS, BLK, HD), bf)
    two = lambda shape, kind: [pltpu.VMEM(shape, kind)] * 2
    wide = jax.ShapeDtypeStruct((tok, HEADS * HD), bf)
    home = jax.ShapeDtypeStruct((BLK, KVH * HD), bf)
    results = pl.pallas_call(
        step_kernel,
        out_shape=[big, big, pltpu.VMEM((BLK, KVH * HD), bf), pltpu.VMEM((BLK, KVH * HD), bf)],
        in_specs=[SM, ANY, ANY, ANY, ANY],
        out_specs=[VM] * 4,
        scratch_shapes=[big] * 2
        + [
            pltpu.VMEM((QB, HEADS * BLK, ENTRIES * BLK), bf),
            pltpu.VMEM((QB, HEADS * BLK, 1), f32),
        ]
        + two((HALF, ENTRIES * BLK), f32)
        + two((CHUNK, HD), f32)
        + two((KVH, BLK, HD), bf)
        + two((QB, BLK, HD), bf)
        + two((POOL, BLK, HD), bf)
        + [slots] * 6
        + two((NONE + 1, HD, BLK), bf)
        + two((SUMS, HD, BLK), f32)
        + two((QB, BLK, HD), bf)
        + two((HD, BLK), bf)
        + [
            pltpu.VMEM((ENTRIES * BLK, HD), bf),
            pltpu.VMEM((HD, ENTRIES * BLK), f32),
            pltpu.SMEM((CTX * SLOTS,), jnp.int32),
            pltpu.SMEM((CTX * SLOTS,), jnp.int32),
            pltpu.SMEM((QB * ENTRIES,), jnp.int32),
        ]
        + [DMA((2, KVH))] * 2
        + [DMA((2, CTX))] * 2
        + [DMA((2, KVH))] * 2
        + [DMA((2, CTX))] * 2
        + [DMA((2,))] * 5
        + [DMA((2, KVH))],
        compiler_params=pltpu.CompilerParams(
            collective_id=0, has_side_effects=True, vmem_limit_bytes=VMEM_BYTES
        ),
    )(random_blocks.T, queries, out_grad, keys, values)
    return pl.pallas_call(
        copy_kernel,
        out_shape=[wide, wide, home, home],
        in_specs=[VM] * 4,
        out_specs=[ANY] * 4,
        scratch_shapes=[DMA((4,))],
        compiler_params=pltpu.CompilerParams(vmem_limit_bytes=2**20),
    )(*[pltpu.with_memory_space_constraint(x, pltpu.VMEM) for x in results])


def solution(mesh):
    in_specs = (
        P("ctx", "kvh"),
        P(("ctx", "kvh"), None),
        P(("ctx", "kvh"), None),
        P("ctx", "kvh"),
        P(),
    )
    out_specs = (P("ctx", "kvh"), P("ctx", "kvh"), P(("ctx", "kvh"), None), P(("ctx", "kvh"), None))
    return jax.shard_map(
        per_device, mesh=mesh, in_specs=in_specs, out_specs=out_specs, check_vma=False
    )
```

```python
import functools

import jax
import jax.numpy as jnp
from jax import lax
from jax.experimental import pallas as pl
from jax.experimental.pallas import tpu as pltpu
from jax.sharding import PartitionSpec as P

HD = 128
BLK = 128
GLOB = 2
RAND = 3
QB = 8
CTX = 16
KVH = 8
HEADS = 8
SLOTS = 2
NKB = QB * CTX
LAG = 4
SIDE = 4
EXTRA = QB
RECV = QB + 1
POOL = RECV + CTX * SLOTS
ENTRIES = 3 + GLOB + RAND
CHUNK = 256
PER = CHUNK // BLK
UNITS = HEADS // PER
PAIR = 2 * PER
HALF = 2 * CHUNK
NAMED = QB * RAND
EDGE = NAMED + GLOB
NONE = EDGE + 2
SUMS = QB + 2 + GLOB
SCALE = HD**-0.5
LOG2E = 1.4426950408889634
MASKED = 1e30
MESH = pl.DeviceIdType.MESH
ORDER = (
    (0, 1), (1, 0), (0, 3), (3, 0), (1, 1), (2, 0), (3, 3), (0, 2),
    (1, 3), (2, 1), (3, 1), (1, 2), (2, 3), (3, 2), (2, 2),
)

NT = (((1,), (1,)), ((), ()))
TN = (((0,), (0,)), ((), ()))


def mm(a, b, dims=(((1,), (0,)), ((), ()))):
    return lax.dot_general(a, b, dims, preferred_element_type=jnp.float32)


def ctx_at(me, dz, dx):
    return lax.rem(me // SIDE + dz, SIDE) * SIDE + lax.rem(me % SIDE + dx, SIDE)


def pick(rand, row, owner, name):
    first = second = jnp.int32(name(None, None))
    count = jnp.int32(0)
    for n in range(NAMED):
        r = rand[n % RAND, row * QB + n // RAND]
        hit = (r >> 3) == owner
        first = jnp.where(hit & (count == 0), name(r, n), first)
        second = jnp.where(hit & (count == 1), name(r, n), second)
        count = count + hit.astype(jnp.int32)
    return first, second


def send_table(rand, me, table):
    def body(dest, carry):
        first, second = pick(rand, dest, me, lambda r, n: 0 if r is None else r & 7)
        first = jnp.where(dest == me + 1, QB - 1, first)
        table[dest * 2] = jnp.where(me == 0, 0, first)
        table[dest * 2 + 1] = jnp.where(me == 0, 1, second)
        return carry

    lax.fori_loop(0, CTX, body, 0)


def back_table(rand, me, table):
    def body(src, carry):
        first, second = pick(rand, me, src, lambda r, n: NONE if r is None else n)
        first = jnp.where(src == me - 1, EDGE, first)
        first = jnp.where(src == me + 1, EDGE + 1, first)
        table[src * 2] = jnp.where(src == 0, NAMED, first)
        table[src * 2 + 1] = jnp.where(src == 0, NAMED + 1, second)
        return carry

    lax.fori_loop(0, CTX, body, 0)


def place_table(rand, me, table):
    def body(i, carry):
        for e in range(3):
            gid = me * QB + i - 1 + e
            near = i - 1 + e
            before = jnp.where(me == 1, EXTRA, RECV + (me - 1) * SLOTS)
            after = RECV + (me + 1) * SLOTS
            place = jnp.where(near < 0, before, jnp.where(near >= QB, after, near))
            ok = (gid >= GLOB) & (gid < NKB)
            table[i * ENTRIES + e] = jnp.where(ok, place, jnp.where(me == 0, 0, RECV))
        for e in range(GLOB):
            table[i * ENTRIES + 3 + e] = jnp.where(me == 0, e, RECV + e)
        for e in range(RAND):
            owner = rand[e, me * QB + i] >> 3
            rank = jnp.int32(0)
            for n in range(NAMED):
                same = ((rand[n % RAND, me * QB + n // RAND] >> 3) == owner) & (n < i * RAND + e)
                rank = rank + same.astype(jnp.int32)
            table[i * ENTRIES + 3 + GLOB + e] = RECV + owner * SLOTS + rank
        return carry

    lax.fori_loop(0, QB, body, 0)


def greet(me, h):
    barrier = pltpu.get_barrier_semaphore()
    for dz, dx in reversed(ORDER):
        peer = (ctx_at(me, dz, dx), h)
        pl.semaphore_signal(barrier, inc=1, device_id=peer, device_id_type=MESH)
    for dh in range(1, KVH):
        peer = (me, lax.rem(h + dh, KVH))
        pl.semaphore_signal(barrier, inc=1, device_id=peer, device_id_type=MESH)
    return lambda: pl.semaphore_wait(barrier, CTX + KVH - 2)


def remote(src, dst, send, recv, peer):
    return pltpu.make_async_remote_copy(
        src_ref=src, dst_ref=dst, send_sem=send, recv_sem=recv, device_id=peer, device_id_type=MESH
    )


def step_kernel(
    rand, q_hbm, g_hbm, key_ref, value_ref,
    o, dq, dk_ref, dv_ref,
    q, g, probs, inverse, left, right, out_left, out_right, heads_k, heads_v, local_k, local_v, pool_k, pool_v, packed_k, packed_v, back_k, back_v,
    arrived_k, arrived_v, terms_k, terms_v, sums_k, sums_v, stage_k, stage_v, extra_k, extra_v,
    listed, part, outgoing, returning, places,
    head_send, head_recv, ctx_send, ctx_recv, home_send, home_recv, ret_send, ret_recv,
    extra_send, extra_recv, own_sem, home_own, in_sem, stage_sem,
):
    me = lax.axis_index("ctx")
    h = lax.axis_index("kvh")
    bf = jnp.bfloat16
    pools, packs, backs = (pool_k, pool_v), (packed_k, packed_v), (back_k, back_v)
    local = (local_k, local_v)
    arrived, terms, sums = (arrived_k, arrived_v), (terms_k, terms_v), (sums_k, sums_v)
    stages, extras = (stage_k, stage_v), (extra_k, extra_v)
    met = greet(me, h)
    loads = [
        pltpu.make_async_copy(q_hbm, q, in_sem.at[0]),
        pltpu.make_async_copy(g_hbm, g, in_sem.at[1]),
    ]
    for copy in loads:
        copy.start()
    heads_in = (heads_k, heads_v)
    for t, ref in enumerate((key_ref, value_ref)):
        for head in range(KVH):
            loads.append(
                pltpu.make_async_copy(
                    ref.at[:, head * HD : (head + 1) * HD], heads_in[t].at[head], stage_sem.at[t, head]
                )
            )
            loads[-1].start()
    met()
    cols = lambda head: pl.ds(pl.multiple_of(head * HD, HD), HD)
    heads = lambda: [(dh, lax.rem(h + dh, KVH)) for dh in range(1, KVH)]
    peers = lambda: [ctx_at(me, dz, dx) for dz, dx in ORDER]
    sent = []
    own = []

    def trail(pack, push):
        order = peers()
        for n in range(len(order) + LAG):
            if n < len(order):
                pack(order[n])
            if n >= LAG:
                push(order[n - LAG])

    def share(t):
        for head in range(KVH):
            loads[2 + t * KVH + head].wait()
        for _, peer in heads():
            sent.append(
                remote(
                    heads_in[t].at[peer], local[t].at[h],
                    head_send.at[t, peer], head_recv.at[t, h], (me, peer),
                )
            )
            sent[-1].start()
        own.append(pltpu.make_async_copy(heads_in[t].at[h], local[t].at[h], own_sem.at[t]))
        own[-1].start()

    share(0)
    send_table(rand, me, outgoing)
    def forward(t):
        own[t].wait()
        for _, peer in heads():
            remote(
                local[t].at[peer], local[t].at[peer],
                head_send.at[t, peer], head_recv.at[t, peer], (me, peer),
            ).wait_recv()

        def pack(peer):
            for k in range(SLOTS):
                packs[t][peer, k] = local[t][outgoing[peer * 2 + k]]

        def push(peer):
            sent.append(
                remote(
                    packs[t].at[peer], pools[t].at[pl.ds(RECV + me * SLOTS, SLOTS)],
                    ctx_send.at[t, peer], ctx_recv.at[t, me], (peer, h),
                )
            )
            sent[-1].start()

        trail(pack, push)
        for b in range(QB):
            pools[t][b] = local[t][b]

        @pl.when(me == 0)
        def _():
            remote(
                local[t].at[QB - 1], pools[t].at[EXTRA], extra_send.at[t], extra_recv.at[t], (1, h)
            ).start()

    forward(0)
    share(1)
    place_table(rand, me, places)
    back_table(rand, me, returning)
    for t in range(2):
        sums[t][...] = jnp.zeros_like(sums[t])
        terms[t][NONE] = jnp.zeros((HD, BLK), bf)
    for copy in loads[:2]:
        copy.wait()

    def arrive(t):
        for peer in peers():
            remote(
                packs[t].at[peer], pools[t].at[pl.ds(RECV + peer * SLOTS, SLOTS)],
                ctx_send.at[t, peer], ctx_recv.at[t, peer], (peer, h),
            ).wait_recv()

        @pl.when(me == 1)
        def _():
            remote(
                local[t].at[QB - 1], pools[t].at[EXTRA], extra_send.at[t], extra_recv.at[t], (0, h)
            ).wait_recv()

    def collect(t, i):
        for e in range(ENTRIES):
            listed[e * BLK : (e + 1) * BLK, :] = pools[t][places[i * ENTRIES + e]]

    def rows_of(i, first, count):
        rows = pl.ds(pl.multiple_of(i * BLK, BLK), BLK)
        return [(rows, slice(n * HD, (n + 1) * HD)) for n in range(first, first + count)]

    def unit(i, u):
        return rows_of(i, u * PER, PER), slice(u * CHUNK, (u + 1) * CHUNK)

    def fold(u, term):
        part[...] = term if u == 1 else part[...] + term

    def stacked(ref, where):
        return jnp.concatenate([ref[w] for w in where], 0)

    def spread(ref, where, value):
        for n, w in enumerate(where):
            ref[w] = value[n * BLK : (n + 1) * BLK].astype(bf)

    def bank(t, i, factor):
        for e in range(ENTRIES):
            term = part[:, e * BLK : (e + 1) * BLK] * factor
            if e < 3:
                sums[t][i + e] += term
            elif e < 3 + GLOB:
                sums[t][QB + 2 + e - 3] += term
            else:
                terms[t][i * RAND + e - 3 - GLOB] = term.astype(bf)

    def give_back(t):
        for n in range(GLOB):
            terms[t][NAMED + n] = sums[t][QB + 2 + n].astype(bf)
        terms[t][EDGE] = sums[t][0].astype(bf)
        terms[t][EDGE + 1] = sums[t][QB + 1].astype(bf)

        @pl.when(me == 0)
        def _():
            for n in range(GLOB):
                sums[t][1 + n] += sums[t][QB + 2 + n]

        def pack(peer):
            for k in range(SLOTS):
                backs[t][peer, k] = terms[t][returning[peer * 2 + k]]

        def push(peer):
            sent.append(
                remote(
                    backs[t].at[peer], arrived[t].at[me],
                    ret_send.at[t, peer], ret_recv.at[t, me], (peer, h),
                )
            )
            sent[-1].start()

        trail(pack, push)

        @pl.when(me == 1)
        def _():
            remote(terms[t].at[EDGE], extras[t], extra_send.at[t], extra_recv.at[t], (0, h)).start()

    def finish(t, ref):
        for dz, dx in ORDER:
            peer = ctx_at(me, SIDE - dz, SIDE - dx)
            remote(
                backs[t].at[peer], arrived[t].at[peer],
                ret_send.at[t, peer], ret_recv.at[t, peer], (peer, h),
            ).wait_recv()
            first = arrived[t][peer, 0].astype(jnp.float32)
            second = arrived[t][peer, 1].astype(jnp.float32)
            for b in range(QB):
                sums[t][1 + b] += first * (outgoing[peer * 2] == b).astype(jnp.float32) + second * (
                    outgoing[peer * 2 + 1] == b
                ).astype(jnp.float32)

        @pl.when(me == 0)
        def _():
            remote(terms[t].at[EDGE], extras[t], extra_send.at[t], extra_recv.at[t], (1, h)).wait_recv()
            sums[t][QB] += extras[t][...].astype(jnp.float32)

        for b in range(QB):
            stages[t][b] = sums[t][1 + b].T.astype(bf)
        for _, peer in heads():
            sent.append(
                remote(
                    stages[t].at[peer], ref.at[:, cols(h)],
                    home_send.at[t, peer], home_recv.at[t, h], (me, peer),
                )
            )
            sent[-1].start()
        own.append(pltpu.make_async_copy(stages[t].at[h], ref.at[:, cols(h)], home_own.at[t]))
        own[-1].start()

    arrive(0)
    forward(1)

    def score(i, u, buf):
        where = rows_of(i, u * PAIR, PAIR)
        buf[...] = mm(stacked(q, where), listed[...], NT)

    def soften(i, u, buf):
        where = rows_of(i, u * PAIR, PAIR)
        span = slice(u * HALF, (u + 1) * HALF)
        s = buf[...]
        top = jnp.max(s, 1, keepdims=True) * (SCALE * LOG2E)
        parts = []
        for e in range(ENTRIES):
            gid = me * QB + i - 1 + e
            ok = (gid >= GLOB) & (gid < NKB)
            base = top + jnp.where(ok, 0.0, MASKED).astype(jnp.float32) if e < 3 else top
            parts.append(jnp.exp2(s[:, e * BLK : (e + 1) * BLK] * (SCALE * LOG2E) - base))
        p = jnp.concatenate(parts, 1)
        inv = 1.0 / jnp.sum(p, 1, keepdims=True)
        probs[i, span] = p.astype(bf)
        inverse[i, span] = inv
        spread(g, where, stacked(g, where).astype(jnp.float32) * inv)

    def both(ref, i, u):
        return stacked(ref, rows_of(i, (u - 1) * PER, 2 * PER))

    def weigh(i, carry):
        following = jnp.minimum(i + 1, QB - 1)
        score(i, 1, right)
        soften(i, 0, left)
        collect(0, following)
        score(following, 0, left)
        soften(i, 1, right)
        part[...] = mm(stacked(g, rows_of(i, 0, HEADS)), probs[i], TN)
        bank(1, i, 1.0)
        return carry

    collect(0, 0)
    score(0, 0, left)
    lax.fori_loop(0, QB, weigh, 0)
    give_back(1)
    arrive(1)

    def project(i, u, buf, out):
        where, span = unit(i, u)
        out[...] = mm(probs[i, span], listed[...])
        buf[:CHUNK] = mm(stacked(g, where), listed[...], NT)

    def grade(i, u, buf, out):
        where, span = unit(i, u)
        value = out[...] * inverse[i, span]
        spread(o, where, value)
        centre = jnp.sum(stacked(g, where).astype(jnp.float32) * value, 1, keepdims=True)
        probs[i, span] = (probs[i, span].astype(jnp.float32) * (buf[:CHUNK] - centre)).astype(bf)

    def blame(i, carry):
        for u in range(UNITS):
            here, there = (left, right) if u % 2 == 0 else (right, left)
            out, ahead = (out_left, out_right) if u % 2 == 0 else (out_right, out_left)
            if u + 1 < UNITS:
                project(i, u + 1, there, ahead)
            else:
                following = jnp.minimum(i + 1, QB - 1)
                collect(1, following)
                project(following, 0, there, ahead)
            grade(i, u, here, out)
            if u % 2 == 1:
                fold(u, mm(both(q, i, u), probs[i, (u - 1) * CHUNK : (u + 1) * CHUNK], TN))
        bank(0, i, SCALE)
        return carry

    collect(1, 0)
    project(0, 0, left, out_left)
    lax.fori_loop(0, QB, blame, 0)
    give_back(0)
    finish(1, dv_ref)

    def steer(i, carry):
        collect(0, i)
        for u in range(1, UNITS, 2):
            where = rows_of(i, (u - 1) * PER, 2 * PER)
            spread(dq, where, mm(probs[i, (u - 1) * CHUNK : (u + 1) * CHUNK], listed[...]) * SCALE)
        return carry

    lax.fori_loop(0, QB, steer, 0)
    finish(0, dk_ref)
    for t in range(2):

        @pl.when(me == 0)
        def _():
            remote(
                local[t].at[QB - 1], pools[t].at[EXTRA], extra_send.at[t], extra_recv.at[t], (1, h)
            ).wait_send()

        @pl.when(me == 1)
        def _():
            remote(terms[t].at[EDGE], extras[t], extra_send.at[t], extra_recv.at[t], (0, h)).wait_send()

    for copy in sent:
        copy.wait_send()
    for copy in own[2:]:
        copy.wait()
    for t, ref in ((1, dv_ref), (0, dk_ref)):
        for _, peer in heads():
            remote(
                stages[t].at[peer], ref.at[:, cols(peer)],
                home_send.at[t, peer], home_recv.at[t, peer], (me, peer),
            ).wait_recv()


def copy_kernel(*refs):
    count = len(refs) // 2
    ins, outs, sem = refs[:count], refs[count : 2 * count], refs[2 * count]
    writes = [
        pltpu.make_async_copy(ins[n], outs[n], sem.at[n]) for n in range(count)
    ]
    for copy in writes:
        copy.start()
    for copy in writes:
        copy.wait()


SM = pl.BlockSpec(memory_space=pltpu.SMEM)
ANY = pl.BlockSpec(memory_space=pl.ANY)
VM = pl.BlockSpec(memory_space=pltpu.VMEM)
DMA = pltpu.SemaphoreType.DMA
VMEM_BYTES = 57 * 2**20


def per_device(queries, keys, values, out_grad, random_blocks):
    bf = jnp.bfloat16
    f32 = jnp.float32
    tok = QB * BLK
    big = pltpu.VMEM((tok, HEADS * HD), bf)
    slots = pltpu.VMEM((CTX, SLOTS, BLK, HD), bf)
    two = lambda shape, kind: [pltpu.VMEM(shape, kind)] * 2
    wide = jax.ShapeDtypeStruct((tok, HEADS * HD), bf)
    home = jax.ShapeDtypeStruct((BLK, KVH * HD), bf)
    results = pl.pallas_call(
        step_kernel,
        out_shape=[big, big, pltpu.VMEM((BLK, KVH * HD), bf), pltpu.VMEM((BLK, KVH * HD), bf)],
        in_specs=[SM, ANY, ANY, ANY, ANY],
        out_specs=[VM] * 4,
        scratch_shapes=[big] * 2
        + [
            pltpu.VMEM((QB, HEADS * BLK, ENTRIES * BLK), bf),
            pltpu.VMEM((QB, HEADS * BLK, 1), f32),
        ]
        + two((HALF, ENTRIES * BLK), f32)
        + two((CHUNK, HD), f32)
        + two((KVH, BLK, HD), bf)
        + two((QB, BLK, HD), bf)
        + two((POOL, BLK, HD), bf)
        + [slots] * 6
        + two((NONE + 1, HD, BLK), bf)
        + two((SUMS, HD, BLK), f32)
        + two((QB, BLK, HD), bf)
        + two((HD, BLK), bf)
        + [
            pltpu.VMEM((ENTRIES * BLK, HD), bf),
            pltpu.VMEM((HD, ENTRIES * BLK), f32),
            pltpu.SMEM((CTX * SLOTS,), jnp.int32),
            pltpu.SMEM((CTX * SLOTS,), jnp.int32),
            pltpu.SMEM((QB * ENTRIES,), jnp.int32),
        ]
        + [DMA((2, KVH))] * 2
        + [DMA((2, CTX))] * 2
        + [DMA((2, KVH))] * 2
        + [DMA((2, CTX))] * 2
        + [DMA((2,))] * 5
        + [DMA((2, KVH))],
        compiler_params=pltpu.CompilerParams(
            collective_id=0, has_side_effects=True, vmem_limit_bytes=VMEM_BYTES
        ),
    )(random_blocks.T, queries, out_grad, keys, values)
    return pl.pallas_call(
        copy_kernel,
        out_shape=[wide, wide, home, home],
        in_specs=[VM] * 4,
        out_specs=[ANY] * 4,
        scratch_shapes=[DMA((4,))],
        compiler_params=pltpu.CompilerParams(vmem_limit_bytes=2**20),
    )(*[pltpu.with_memory_space_constraint(x, pltpu.VMEM) for x in results])


def solution(mesh):
    in_specs = (
        P("ctx", "kvh"),
        P(("ctx", "kvh"), None),
        P(("ctx", "kvh"), None),
        P("ctx", "kvh"),
        P(),
    )
    out_specs = (P("ctx", "kvh"), P("ctx", "kvh"), P(("ctx", "kvh"), None), P(("ctx", "kvh"), None))
    return jax.shard_map(
        per_device, mesh=mesh, in_specs=in_specs, out_specs=out_specs, check_vma=False
    )
```
